512 devices in a mesh: pair: 64 (over x, y, z_hi), sector: 8 (over z_lo, core).
Axes of the slice: x: 4, y: 4, z: 16 (z_hi: 4, z_lo: 4; z = z_hi * 4 + z_lo), core: 2. Of those that a mesh axis runs over, the one named last changes fastest.
Arguments:
- site_tensor: bfloat16 [4, 16, 128, 128], P(None, 'sector', 'pair'), may hold values from -0.5 to 0.5
- operators: bfloat16 [1536, 16, 128, 128], P('pair', 'sector'), may hold values from -6 to 6
- one_index: bfloat16 [128, 16, 128, 128], P('pair', 'sector'), may hold values from -6 to 6
- weights: bfloat16 [1536, 128], P('pair'), may hold values from -1 to 1
- comp_charge: int32 [1536], P('pair'), may hold values from 0 to 2
- one_charge: int32 [128], replicated, may hold values from 0 to 2
- sector_size: int32 [16], replicated, may hold values from 1 to 128, 1280 in all
- coupling: int32 [16, 4], replicated, may hold values from 0 to 16, as said below
Outputs:
- renormalized: bfloat16 [1536, 16, 128, 128], P('pair', 'sector')
The draws below stay inside these ranges and needn't reach their ends.
Inputs may be any that keep to these rules, and one draw needn't show every extreme that they name: coupling[s, t] = min(s + c[t], 16) where c is an arrangement of the charges 0, 1, 1, 2 over the 4 orbital states; the value 16 marks a dropped combination.
All inputs are finite; a program needn't handle non-finite values.
Results may differ from the reference program's by a relative error of at most 0.007.
Values may be sent and summed in bfloat16 or wider, within the bound.
No kernel may reach another device: no remote copies, remote signals or barrier semaphores. Data moves between devices by JAX's collectives and lax.ppermute only.
A program may use at most 64 MiB of HBM per device.

```python
import math
import jax
import jax.numpy as jnp
import numpy as np
from jax import lax

S = 16
B = 128
DLOC = 4
OPERATORS = 1536
ONE_OPS = 128


def draw_coupling(key, part):
    order = jax.random.permutation(jax.random.fold_in(key, 7), DLOC)
    charge_table = jnp.array([0, 1, 1, 2], jnp.int32)
    charges = jnp.take(charge_table, order)
    sectors = jnp.arange(S, dtype=jnp.int32)[:, None]
    return jnp.minimum(sectors + charges[None, :], S).astype(jnp.int32)


def plant(values, rng, low, largest):
    extent = values.shape
    place = [jax.random.randint(jax.random.fold_in(rng, axis), (), 0, extent[axis]) for axis in range(len(extent))]
    values = values.at[tuple(place)].set(low)
    longest = extent.index(max(extent))
    place[longest] = (place[longest] + 1) % extent[longest]
    return values.at[tuple(place)].set(largest)


def shard_levels(key, extent, shards, low, largest):
    level, own = 1.0, jax.random.fold_in(key, 6)
    for dim, parts in shards:
        steps = jnp.exp(jax.random.uniform(jax.random.fold_in(own, dim), (parts,), jnp.float32, low / len(shards), largest / len(shards)))
        level = level * jnp.repeat(steps, extent[dim] // parts).reshape([-1 if axis == dim else 1 for axis in range(len(extent))])
    return level


def length_profile(count, total, bound, lean):
    loads = [(1 << 20) // math.isqrt(grade ** lean) + 1 for grade in range(2, count + 1)]
    surplus, holding = total - bound - (count - 1), [1] * (count - 1)
    while surplus > 0:
        movable = [i for i in range(count - 1) if holding[i] < bound]
        pool, remaining = sum([loads[i] for i in movable]), surplus
        for i in movable:
            addition = min(bound - holding[i], max(1, remaining * loads[i] // pool), surplus)
            holding[i] = holding[i] + addition
            surplus = surplus - addition
    return np.array([bound] + holding)


def ragged(own_key, number_of, total, reach, skew):
    if number_of == 2:
        one = jax.random.randint(own_key, (), max(1, total - reach), min(reach, total - 1) + 1)
        return jnp.stack([one, total - one])
    sizes = jnp.asarray(length_profile(number_of, total, reach, skew), jnp.int32)
    pairs = (number_of - 1) // 2
    source_of, sink = sizes[1:1 + 2 * pairs:2], sizes[2:2 + 2 * pairs:2]
    slack = jnp.minimum(source_of - 1, reach - sink)
    passed = jax.random.randint(jax.random.fold_in(own_key, 1), (pairs,), 0, 1 << 20) % (slack + 1)
    sizes = sizes.at[1:1 + 2 * pairs:2].set(source_of - passed).at[2:2 + 2 * pairs:2].set(sink + passed)
    return sizes[jax.random.permutation(jax.random.fold_in(own_key, 2), number_of)]


def bell_draw(own_key, shape, scale, most, pieces=(), kind=jnp.bfloat16):
    values = scale * jax.random.normal(own_key, shape, jnp.float32)
    if pieces:
        values = values * shard_levels(own_key, shape, pieces, -0.22, 0.18)
    return jnp.clip(values, -most, most).astype(kind)


def setup_inputs(seed: int = 0) -> dict:
    key_list = jax.random.split(jax.random.key(seed), 9)
    return {
        "site_tensor": bell_draw(key_list[0], (DLOC, S, B, B), B ** -0.5, 0.5, ((1, 8), (2, 64))),
        "operators": bell_draw(key_list[1], (OPERATORS, S, B, B), 1.0, 6.0, ((0, 64), (1, 8))),
        "one_index": bell_draw(key_list[2], (ONE_OPS, S, B, B), 1.0, 6.0, ((0, 64), (1, 8))),
        "weights": bell_draw(key_list[3], (OPERATORS, ONE_OPS), (ONE_OPS // 3) ** -0.5, 1.0, ((0, 64),)),
        "comp_charge": plant(jax.random.randint(key_list[4], (OPERATORS,), 0, 3), jax.random.fold_in(key_list[4], 1), 0, 2).astype(jnp.int32),
        "one_charge": plant(jax.random.randint(key_list[5], (ONE_OPS,), 0, 3), jax.random.fold_in(key_list[5], 1), 0, 2).astype(jnp.int32),
        "sector_size": ragged(key_list[6], S, S * B * 5 // 8, B, 1).astype(jnp.int32),
        "coupling": draw_coupling(jax.random.fold_in(key_list[8], 71), 0),
    }


def reference(site_tensor, operators, one_index, weights, comp_charge, one_charge, sector_size, coupling):
    positions = jnp.arange(B, dtype=jnp.int32)
    live_rows = positions[None, :] < sector_size[:, None]
    masked = jnp.where(live_rows[None, :, :, None], site_tensor, jnp.zeros((), jnp.bfloat16))
    matching = comp_charge[:, None] == one_charge[None, :]
    coef = jnp.where(matching, weights, jnp.zeros((), jnp.bfloat16))

    def build(sector):
        own_ops = operators[:, sector]
        own_one = one_index[:, sector]
        summed = jnp.dot(coef, own_one.reshape(ONE_OPS, B * B), preferred_element_type=jnp.float32)
        return (own_ops.astype(jnp.float32) + summed.reshape(OPERATORS, B, B)).astype(jnp.bfloat16)

    combined = lax.map(build, jnp.arange(S, dtype=jnp.int32))
    state_charge = coupling[0]

    def new_sector(target):
        total = jnp.zeros((OPERATORS, B, B), jnp.float32)
        for local_state in range(DLOC):
            source = target - state_charge[local_state]
            usable = source >= 0
            clipped = jnp.clip(source, 0, S - 1).astype(jnp.int32)
            left_block = masked[local_state, clipped]
            right_index = clipped + comp_charge
            in_range = right_index < S
            right_blocks = masked[local_state, jnp.clip(right_index, 0, S - 1).astype(jnp.int32)]
            right_blocks = jnp.where(in_range[:, None, None], right_blocks, jnp.zeros((), jnp.bfloat16))
            partial_value = jnp.einsum("kij,kjc->kic", combined[clipped].astype(jnp.float32), right_blocks.astype(jnp.float32), precision=lax.Precision.HIGHEST).astype(jnp.bfloat16)
            contrib = jnp.einsum("ia,kic->kac", left_block.astype(jnp.float32), partial_value.astype(jnp.float32), precision=lax.Precision.HIGHEST)
            total = total + jnp.where(usable, contrib, jnp.zeros((), jnp.float32))
        return total.astype(jnp.bfloat16)

    result = lax.map(new_sector, jnp.arange(S, dtype=jnp.int32))
    return jnp.transpose(result, (1, 0, 2, 3))
```

```python
import functools
import jax
import jax.numpy as jnp
from jax import lax
from jax.experimental import pallas as pl
from jax.experimental.pallas import tpu as pltpu
from jax.sharding import Mesh, PartitionSpec as P

F32 = jnp.float32
BF16 = jnp.bfloat16
PLANE = ("x", "y")
GROUP = ("zl", "core")
VMEM = pl.BlockSpec(memory_space=pltpu.VMEM)
SMEM = pl.BlockSpec(memory_space=pltpu.SMEM)


def call(body, out, ins, name, scratch=(), flops=0, moved=4 << 20):
    return pl.pallas_call(
        body,
        out_shape=out,
        in_specs=ins,
        out_specs=jax.tree.map(lambda _: VMEM, out),
        scratch_shapes=list(scratch),
        name=name,
        cost_estimate=pl.CostEstimate(flops=flops, bytes_accessed=moved, transcendentals=0),
        compiler_params=pltpu.CompilerParams(vmem_limit_bytes=40 << 20),
    )


def shift(value, steps):
    count = 8
    first, last = max(0, -steps), min(count, count - steps)
    return lax.ppermute(value, GROUP, [(a, a + steps) for a in range(first, last)])


def pack_kernel(comp_ref, one_ref, w_ref, o_ref, out_ref):
    planes = out_ref.shape[0]
    for j in range(2):
        parts = [o_ref[j, s].astype(F32).reshape(planes, 8, 128) for s in range(2)]
        out_ref[:, j * 16 : (j + 1) * 16, :] = jnp.concatenate(parts, axis=1).astype(BF16)
    ops = w_ref.shape[0]
    row = lax.broadcasted_iota(jnp.int32, (ops, 128), 0)
    charge = jnp.zeros((ops, 128), jnp.int32)
    for k in range(ops):
        charge = jnp.where(row == k, comp_ref[k], charge)
    match = charge == jnp.broadcast_to(one_ref[...], (ops, 128))
    coef = jnp.where(match, w_ref[...].astype(F32), 0.0).astype(BF16)
    for d in range(planes):
        out_ref[d, 32 : 32 + ops, :] = coef


def mix_kernel(a_ref, g_ref, out_ref, gf_ref, cf_ref, sf_ref):
    planes = a_ref.shape[0]
    ops = a_ref.shape[1] - 32
    for zh in range(4):
        for p in range(planes):
            at = (p * 4 + zh) * 32
            gf_ref[at : at + 32, :] = g_ref[zh, p * 32 : (p + 1) * 32, :].astype(F32)
    coef = a_ref[:, 32 : 32 + ops, :].astype(F32).reshape(planes * ops, 128).astype(BF16)
    for q in range(16):
        block = gf_ref[pl.ds(q, 128, stride=16), :].astype(BF16)
        cf_ref[pl.ds(q, planes * ops, stride=16), :] = jnp.dot(coef, block, preferred_element_type=F32)
    rows = ops * 16
    for zh in range(4):
        piece = g_ref[zh, planes * 32 : planes * 32 + 16, :].astype(F32)
        for b in range(8):
            sf_ref[b * 8 + zh * 2 : b * 8 + zh * 2 + 2, :] = piece[2 * b : 2 * b + 2, :]
    site = sf_ref[...].astype(BF16)

    def finish(d, _):
        at = pl.multiple_of(d * rows, 16)
        out_ref[d, :rows, :] = cf_ref[pl.ds(at, rows), :].astype(BF16)
        out_ref[d, rows:, :] = site
        return 0

    lax.fori_loop(0, planes, finish, 0)


def state_order(coupling_ref):
    c = [coupling_ref[0, t] for t in range(4)]
    zero, two, one_low, one_high = (jnp.int32(0) for _ in range(4))
    for t in range(4):
        zero = jnp.where(c[t] == 0, t, zero)
        two = jnp.where(c[t] == 2, t, two)
        one_high = jnp.where(c[t] == 1, t, one_high)
    for t in reversed(range(4)):
        one_low = jnp.where(c[t] == 1, t, one_low)
    return [zero, one_low, one_high, two]


def site_kernel(coupling_ref, size_ref, r_ref, out_ref):
    rows = r_ref.shape[1] - 64
    first = 4 * lax.axis_index("zl") + 2 * lax.axis_index("core")
    line = lax.broadcasted_iota(jnp.int32, (128, 128), 0)
    order = state_order(coupling_ref)
    for n in range(4):
        at = pl.multiple_of(rows + order[n] * 16, 16)
        both = r_ref[:, pl.ds(at, 16), :].astype(F32)
        for s in range(2):
            block = both[:, s * 8 : (s + 1) * 8, :].reshape(128, 128)
            out_ref[s, n] = jnp.where(line < size_ref[first + s], block, 0.0).astype(BF16)


def combine_kernel(r_ref, op_ref, out_ref):
    def step(k, _):
        at = pl.multiple_of(k * 16, 16)
        both = r_ref[:, pl.ds(at, 16), :].astype(F32)
        for s in range(2):
            summed = both[:, s * 8 : (s + 1) * 8, :].reshape(128, 128)
            out_ref[k, s] = (op_ref[k, s].astype(F32) + summed).astype(BF16)
        return 0

    lax.fori_loop(0, op_ref.shape[0], step, 0, unroll=2)


def lay_pool(own_ref, up_ref, pool_ref, states):
    for p in range(4):
        source = own_ref if p < 2 else up_ref
        for at, n in enumerate(states):
            pool_ref[p, :, at * 128 : (at + 1) * 128] = source[p % 2, n]


def turned(ref, s, n):
    return ref[s, n].astype(F32).T.astype(BF16)


def carry_kernel(charge_ref, own_ref, up_ref, comb_ref, out_ref, pool_ref, left_ref):
    lay_pool(own_ref, up_ref, pool_ref, (1, 2, 3))
    left_ref[:, 0:128] = turned(own_ref, 1, 1)
    left_ref[:, 128:256] = turned(own_ref, 1, 2)
    left_ref[:, 256:384] = turned(own_ref, 0, 3)
    left_ref[:, 384:512] = turned(own_ref, 1, 3)

    def step(h, _):
        top, low = [], []
        for e in range(2):
            k = 2 * h + e
            q = charge_ref[k]
            one = jnp.dot(comb_ref[k, 1], pool_ref[q + 1], preferred_element_type=F32).astype(BF16)
            zero = jnp.dot(comb_ref[k, 0], pool_ref[q, :, 256:], preferred_element_type=F32).astype(BF16)
            top.append(jnp.concatenate([one[:, :128], one[:, 128:256], zero], axis=0))
            low.append(one[:, 256:])
        u2 = jnp.dot(left_ref[:, :384], jnp.concatenate(top, axis=1), preferred_element_type=F32)
        u3 = jnp.dot(left_ref[:, 384:], jnp.concatenate(low, axis=1), preferred_element_type=F32)
        for e in range(2):
            out_ref[2 * h + e, 0] = u2[:, e * 128 : (e + 1) * 128].astype(BF16)
            out_ref[2 * h + e, 1] = u3[:, e * 128 : (e + 1) * 128].astype(BF16)
        return 0

    lax.fori_loop(0, comb_ref.shape[0] // 2, step, 0, unroll=2)


def own_kernel(charge_ref, own_ref, up_ref, comb_ref, out_ref, pool_ref, left_ref):
    lay_pool(own_ref, up_ref, pool_ref, (0, 1, 2))
    left_ref[:, 0:128] = turned(own_ref, 0, 1)
    left_ref[:, 128:256] = turned(own_ref, 0, 2)
    left_ref[:, 256:384] = turned(own_ref, 1, 0)
    left_ref[:, 384:512] = turned(own_ref, 0, 0)

    def step(h, _):
        top, low = [], []
        for e in range(2):
            k = 2 * h + e
            q = charge_ref[k]
            zero = jnp.dot(comb_ref[k, 0], pool_ref[q], preferred_element_type=F32).astype(BF16)
            one = jnp.dot(comb_ref[k, 1], pool_ref[q + 1, :, :128], preferred_element_type=F32).astype(BF16)
            top.append(jnp.concatenate([zero[:, 128:256], zero[:, 256:], one], axis=0))
            low.append(zero[:, :128])
        u1 = jnp.dot(left_ref[:, :384], jnp.concatenate(top, axis=1), preferred_element_type=F32)
        u0 = jnp.dot(left_ref[:, 384:], jnp.concatenate(low, axis=1), preferred_element_type=F32)
        for e in range(2):
            out_ref[2 * h + e, 0] = u0[:, e * 128 : (e + 1) * 128]
            out_ref[2 * h + e, 1] = u1[:, e * 128 : (e + 1) * 128]
        return 0

    lax.fori_loop(0, comb_ref.shape[0] // 2, step, 0, unroll=2)


def body(site_tensor, operators, one_index, weights, comp_charge, one_charge, sector_size, coupling):
    ops = operators.shape[0]
    rows = ops * 16
    sds = jax.ShapeDtypeStruct
    message = call(pack_kernel, sds((16, 32 + ops, 128), BF16), [SMEM, VMEM, VMEM, VMEM], "pack")(
        comp_charge, one_charge.reshape(1, 128), weights, one_index
    )
    near = lax.all_to_all(message, PLANE, 0, 0, tiled=True)
    column = jnp.concatenate([near[:, :32].reshape(512, 128), site_tensor.reshape(16, 128)], axis=0)
    far = lax.all_gather(column, "zh", axis=0)
    mixed = call(
        mix_kernel,
        sds((16, rows + 64, 128), BF16),
        [VMEM, VMEM],
        "mix",
        [pltpu.VMEM((2048, 128), F32), pltpu.VMEM((16 * rows, 128), F32), pltpu.VMEM((64, 128), F32)],
    )(near, far)
    landed = lax.all_to_all(mixed, PLANE, 0, 0, tiled=True)
    own = call(site_kernel, sds((2, 4, 128, 128), BF16), [SMEM, SMEM, VMEM], "site")(
        coupling, sector_size, landed
    )
    upper = shift(own, -1)
    comb = call(combine_kernel, sds((ops, 2, 128, 128), BF16), [VMEM, VMEM], "combine")(landed, operators)
    scratch = [pltpu.VMEM((4, 128, 384), BF16), pltpu.VMEM((128, 512), BF16)]
    flops = ops * 4 * 2 * 2 * 128**3
    ins = [SMEM, VMEM, VMEM, VMEM]
    leaving = call(carry_kernel, sds((ops, 2, 128, 128), BF16), ins, "carry", scratch, flops)(
        comp_charge, own, upper, comb
    )
    carried = shift(leaving, 1)
    kept = call(own_kernel, sds((ops, 2, 128, 128), F32), ins, "own", scratch, flops)(
        comp_charge, own, upper, comb
    )
    return (kept + carried.astype(F32)).astype(BF16)


def solution(mesh):
    fine = Mesh(mesh.devices.reshape(4, 4, 4, 4, 2), ("x", "y", "zh", "zl", "core"))
    pair, sector = ("x", "y", "zh"), ("zl", "core")
    return jax.shard_map(
        body,
        mesh=fine,
        in_specs=(
            P(None, sector, pair, None),
            P(pair, sector, None, None),
            P(pair, sector, None, None),
            P(pair, None),
            P(pair),
            P(),
            P(),
            P(),
        ),
        out_specs=P(pair, sector, None, None),
        check_vma=False,
    )
```

```python
import jax
import jax.numpy as jnp
from jax import lax
from jax.experimental import pallas as pl
from jax.experimental.pallas import tpu as pltpu
from jax.sharding import Mesh, PartitionSpec as P

F32 = jnp.float32
BF16 = jnp.bfloat16
PLANE = ("x", "y")
GROUP = ("zl", "core")
VMEM = pl.BlockSpec(memory_space=pltpu.VMEM)
SMEM = pl.BlockSpec(memory_space=pltpu.SMEM)
HBM = pl.BlockSpec(memory_space=pltpu.MemorySpace.HBM)
DMA = pltpu.SemaphoreType.DMA
COEF_AT, SITE_AT, MESSAGE = 128, 160, 224


def call(body, out, ins, outs, scratch=(), flops=0, moved=4 << 20, grant=16 << 20, **more):
    return pl.pallas_call(
        body,
        out_shape=out,
        in_specs=ins,
        out_specs=outs,
        scratch_shapes=list(scratch),
        cost_estimate=pl.CostEstimate(flops=flops, bytes_accessed=moved, transcendentals=0),
        compiler_params=pltpu.CompilerParams(vmem_limit_bytes=grant),
        **more,
    )


def shift(value, steps):
    count = lax.axis_size(GROUP)
    first, last = max(0, -steps), min(count, count - steps)
    return lax.ppermute(value, GROUP, [(a, a + steps) for a in range(first, last)])


def spread_kernel(c_ref, g_ref, out_ref, sf_ref):
    planes = out_ref.shape[0]
    for half in range(2):
        for zh in range(4):
            parts = []
            for j in range(2):
                at = (j * 2 + 1 - half) * 128
                parts.append(g_ref[zh, at : at + 128, :].astype(F32).reshape(planes, 8, 128))
            to = half * 64 + zh * 16
            out_ref[:, to : to + 16, :] = jnp.concatenate(parts, axis=1).astype(BF16)
    for zh in range(4):
        piece = g_ref[zh, 512:528, :].astype(F32)
        for b in range(8):
            sf_ref[b * 8 + zh * 2 : b * 8 + zh * 2 + 2, :] = piece[2 * b : 2 * b + 2, :]
    site = sf_ref[...].astype(BF16)
    coef = c_ref[...].astype(F32)
    coef = jnp.concatenate([coef, jnp.zeros((SITE_AT - COEF_AT - c_ref.shape[0], 128), F32)], axis=0).astype(BF16)
    for d in range(planes):
        out_ref[d, COEF_AT:SITE_AT, :] = coef
        out_ref[d, SITE_AT:, :] = site


def mix(half, a_ref, out_ref, gf_ref, cf_ref):
    planes, rows = out_ref.shape[:2]
    ops = rows // 8
    coef = a_ref[:, COEF_AT : COEF_AT + ops, :].astype(F32).reshape(planes * ops, 128).astype(BF16)
    gf_ref[...] = a_ref[:, half * 64 : half * 64 + 64, :].astype(F32).reshape(1024, 128)
    for r in range(8):
        block = gf_ref[pl.ds(r, 128, stride=8), :].astype(BF16)
        cf_ref[pl.ds(r, planes * ops, stride=8), :] = jnp.dot(coef, block, preferred_element_type=F32)

    def finish(d, _):
        at = pl.multiple_of(d * rows, 16)
        out_ref[d] = cf_ref[pl.ds(at, rows), :].astype(BF16)
        return 0

    lax.fori_loop(0, planes, finish, 0, unroll=4)


def mix_one(*refs):
    mix(0, *refs)


def mix_zero(*refs):
    mix(1, *refs)


def state_order(coupling_ref):
    c = [coupling_ref[0, t] for t in range(4)]
    zero, two, low, high = (jnp.int32(0) for _ in range(4))
    for t in range(4):
        zero = jnp.where(c[t] == 0, t, zero)
        two = jnp.where(c[t] == 2, t, two)
        high = jnp.where(c[t] == 1, t, high)
    for t in reversed(range(4)):
        low = jnp.where(c[t] == 1, t, low)
    return [zero, low, high, two]


def site_kernel(coupling_ref, size_ref, a_ref, own_ref):
    first = 4 * lax.axis_index("zl") + 2 * lax.axis_index("core")
    line = lax.broadcasted_iota(jnp.int32, (128, 128), 0)
    order = state_order(coupling_ref)
    for n in range(4):
        at = pl.multiple_of(SITE_AT + order[n] * 16, 16)
        both = a_ref[:, pl.ds(at, 16), :].astype(F32)
        for s in range(2):
            block = both[:, s * 8 : (s + 1) * 8, :].reshape(128, 128)
            block = jnp.where(line < size_ref[first + s], block, 0.0)
            own_ref[s, :, n * 128 : (n + 1) * 128] = block.astype(BF16)


def combine(r_ref, own, h):
    both = r_ref[:, pl.ds(pl.multiple_of(h * 16, 16), 16), :].astype(F32)
    pair = []
    for e in range(2):
        summed = both[:, e * 8 : (e + 1) * 8, :].reshape(128, 128)
        pair.append((own[e].astype(F32) + summed).astype(BF16))
    return pair


def inner(block, right):
    return jnp.dot(block, right, preferred_element_type=F32).astype(BF16)


def joined(parts, first, last):
    return jnp.concatenate([v[:, first:last] for v in parts], axis=1)


def stacked(parts, first):
    tall = [jnp.concatenate([v[:, first : first + 128], v[:, first + 128 : first + 256]], axis=0) for v in parts]
    return jnp.concatenate(tall, axis=1)


def product(left, right):
    return jnp.dot(left, right, preferred_element_type=F32)


def pool_kernel(own_ref, up_ref, pool_ref, again_ref):
    for ref in (pool_ref, again_ref):
        for s in range(2):
            ref[s] = own_ref[s]
            ref[2 + s] = up_ref[s]


def turned(pool_ref, s, states):
    blocks = [pool_ref[s, :, n * 128 : (n + 1) * 128].astype(F32).T for n in states]
    return jnp.concatenate(blocks, axis=1).astype(BF16)


def front_kernel(charge_ref, r_ref, op_ref, pool_ref, out_ref, comb_ref, last_ref, left_ref):
    left_ref[...] = turned(pool_ref, 1, (3,))
    last_ref[:3] = pool_ref[:3, :, 384:]
    last_ref[3] = turned(pool_ref, 0, (3,))

    def step(h, _):
        pair = combine(r_ref, [op_ref[2 * h + e] for e in range(2)], h)
        parts = []
        for e in range(2):
            comb_ref[2 * h + e] = pair[e]
            parts.append(inner(pair[e], pool_ref[charge_ref[2 * h + e] + 1, :, 384:]))
        two = product(left_ref[...], joined(parts, 0, 128))
        for e in range(2):
            out_ref[2 * h + e] = two[:, e * 128 : (e + 1) * 128].astype(BF16)
        return 0

    lax.fori_loop(0, op_ref.shape[0] // 2, step, 0, unroll=4)


def middle_kernel(charge_ref, comb_ref, pool_ref, next_ref, left_ref):
    left_ref[...] = turned(pool_ref, 1, (1, 2))

    def step(h, _):
        parts = [inner(comb_ref[2 * h + e], pool_ref[charge_ref[2 * h + e] + 1, :, 128:384]) for e in range(2)]
        one = product(left_ref[...], stacked(parts, 0))
        for e in range(2):
            next_ref[2 * h + e] = one[:, e * 128 : (e + 1) * 128]
        return 0

    lax.fori_loop(0, comb_ref.shape[0] // 2, step, 0, unroll=4)


def last_kernel(charge_ref, r_ref, op_ref, next_ref, last_ref, out_ref, comb_ref):
    def step(h, _):
        pair = combine(r_ref, [op_ref[2 * h + e] for e in range(2)], h)
        parts = []
        for e in range(2):
            comb_ref[2 * h + e] = pair[e]
            parts.append(inner(pair[e], last_ref[charge_ref[2 * h + e]]))
        two = product(last_ref[3], joined(parts, 0, 128))
        for e in range(2):
            k = 2 * h + e
            out_ref[k] = (two[:, e * 128 : (e + 1) * 128] + next_ref[k]).astype(BF16)
        return 0

    lax.fori_loop(0, op_ref.shape[0] // 2, step, 0, unroll=6)


def own_kernel(charge_ref, one_ref, zero_ref, pool_ref, first_ref, second_ref, left_ref):
    left_ref[...] = jnp.concatenate([turned(pool_ref, 0, (0, 1, 2)), turned(pool_ref, 1, (0,))], axis=1)

    def step(h, _):
        low, high = [], []
        for e in range(2):
            k = 2 * h + e
            q = charge_ref[k]
            low.append(inner(zero_ref[k], pool_ref[q, :, :384]))
            high.append(inner(one_ref[k], pool_ref[q + 1, :, :128]))
        first = product(left_ref[:, :128], joined(low, 0, 128))
        second = product(left_ref[:, 128:384], stacked(low, 128)) + product(left_ref[:, 384:], joined(high, 0, 128))
        for e in range(2):
            k, at = 2 * h + e, slice(e * 128, (e + 1) * 128)
            first_ref[k] = first[:, at]
            second_ref[k] = second[:, at]
        return 0

    lax.fori_loop(0, one_ref.shape[0] // 2, step, 0, unroll=2)


def close(sector, kept_ref, came_ref, out_hbm, done_ref, sems):
    size = kept_ref.shape[0] // 3
    moves = []
    for piece in range(3):
        at = slice(piece * size, (piece + 1) * size)
        done_ref[at] = (kept_ref[at] + came_ref[at].astype(F32)).astype(BF16)
        moves.append(pltpu.make_async_copy(done_ref.at[at], out_hbm.at[at, sector], sems.at[piece]))
        moves[-1].start()
    for move in moves:
        move.wait()


def close_one(kept_ref, came_ref, out_hbm, done_ref, sems):
    close(1, kept_ref, came_ref, out_hbm, done_ref, sems)


def close_zero(kept_ref, came_ref, _, out_hbm, done_ref, sems):
    close(0, kept_ref, came_ref, out_hbm, done_ref, sems)


def body(site_tensor, operators, one_index, weights, comp_charge, one_charge, sector_size, coupling):
    ops = operators.shape[0]
    sds = jax.ShapeDtypeStruct
    column = jnp.concatenate([one_index.reshape(512, 128), site_tensor.reshape(16, 128)], axis=0)
    far = lax.all_gather(column, "zh", axis=0)
    coef = jnp.where(comp_charge[:, None] == one_charge[None, :], weights, jnp.zeros((), BF16))
    message = call(
        spread_kernel, sds((16, MESSAGE, 128), BF16), [VMEM, VMEM], VMEM, [pltpu.VMEM((64, 128), F32)]
    )(coef, far)
    near = lax.all_to_all(message, PLANE, 0, 0, tiled=True)
    rows = ops * 8
    mixed = sds((16, rows, 128), BF16)
    scratch = [pltpu.VMEM((1024, 128), F32), pltpu.VMEM((16 * rows, 128), F32)]
    flops = 2 * ops * 2 * 128**3
    half, wide, site = sds((ops, 128, 128), BF16), sds((ops, 128, 128), F32), sds((2, 128, 512), BF16)
    mixed_one = call(mix_one, mixed, [VMEM], VMEM, scratch)(near)
    landed_one = lax.all_to_all(mixed_one, PLANE, 0, 0, tiled=True)
    own = call(site_kernel, site, [SMEM, SMEM, VMEM], VMEM)(coupling, sector_size, near)
    upper = shift(own, -1)
    pool, again = call(pool_kernel, [sds((4, 128, 512), BF16)] * 2, [VMEM] * 2, [VMEM] * 2)(own, upper)
    mixed_zero = call(mix_zero, mixed, [VMEM], VMEM, scratch)(near)
    zero, one = operators[:, 0], operators[:, 1]
    landed_zero = lax.all_to_all(mixed_zero, PLANE, 0, 0, tiled=True)
    leave, comb_one, last = call(
        front_kernel,
        [half, half, sds((4, 128, 128), BF16)],
        [SMEM] + [VMEM] * 3,
        [VMEM] * 3,
        [pltpu.VMEM((128, 128), BF16)],
        flops=flops,
    )(comp_charge, landed_one, one, pool)
    came_one = shift(leave, 1)
    toward = call(
        middle_kernel, wide, [SMEM] + [VMEM] * 2, VMEM, [pltpu.VMEM((128, 256), BF16)], flops=2 * flops
    )(comp_charge, comb_one, pool)
    leave, comb_zero = call(last_kernel, [half, half], [SMEM] + [VMEM] * 4, [VMEM] * 2, flops=flops)(
        comp_charge, landed_zero, zero, toward, last
    )
    came_zero = shift(leave, 1)
    first, second = call(
        own_kernel, [wide, wide], [SMEM] + [VMEM] * 3, [VMEM] * 2, [pltpu.VMEM((128, 512), BF16)], flops=4 * flops
    )(comp_charge, comb_one, comb_zero, again)
    whole = sds((ops, 2, 128, 128), BF16)
    scratch = [pltpu.VMEM((ops, 128, 128), BF16), DMA((3,))]
    out = call(close_one, whole, [VMEM] * 2, HBM, scratch)(second, came_one)
    return call(close_zero, whole, [VMEM, VMEM, HBM], HBM, scratch, input_output_aliases={2: 0})(first, came_zero, out)


def solution(mesh):
    fine = Mesh(mesh.devices.reshape(4, 4, 4, 4, 2), ("x", "y", "zh", "zl", "core"))
    pair, sector = ("x", "y", "zh"), ("zl", "core")
    return jax.shard_map(
        body,
        mesh=fine,
        in_specs=(
            P(None, sector, pair, None),
            P(pair, sector, None, None),
            P(pair, sector, None, None),
            P(pair, None),
            P(pair),
            P(),
            P(),
            P(),
        ),
        out_specs=P(pair, sector, None, None),
        check_vma=False,
    )
```

```python
import jax
import jax.numpy as jnp
from jax import lax
from jax.experimental import pallas as pl
from jax.experimental.pallas import tpu as pltpu
from jax.sharding import Mesh, PartitionSpec as P

F32 = jnp.float32
BF16 = jnp.bfloat16
PLANE = ("x", "y")
GROUP = ("zl", "core")
VMEM = pl.BlockSpec(memory_space=pltpu.VMEM)
SMEM = pl.BlockSpec(memory_space=pltpu.SMEM)
HBM = pl.BlockSpec(memory_space=pltpu.MemorySpace.HBM)
DMA = pltpu.SemaphoreType.DMA
COEF_AT, SITE_AT, MESSAGE = 128, 160, 224


def call(body, out, ins, outs, scratch=(), flops=0, moved=4 << 20, grant=16 << 20, **more):
    return pl.pallas_call(
        body,
        out_shape=out,
        in_specs=ins,
        out_specs=outs,
        scratch_shapes=list(scratch),
        cost_estimate=pl.CostEstimate(flops=flops, bytes_accessed=moved, transcendentals=0),
        compiler_params=pltpu.CompilerParams(vmem_limit_bytes=grant),
        **more,
    )


def shift(value, steps):
    count = lax.axis_size(GROUP)
    first, last = max(0, -steps), min(count, count - steps)
    return lax.ppermute(value, GROUP, [(a, a + steps) for a in range(first, last)])


def spread_kernel(c_ref, g_ref, out_ref, sf_ref):
    planes = out_ref.shape[0]
    for half in range(2):
        for zh in range(4):
            parts = []
            for j in range(2):
                at = (j * 2 + 1 - half) * 128
                parts.append(g_ref[zh, at : at + 128, :].astype(F32).reshape(planes, 8, 128))
            to = half * 64 + zh * 16
            out_ref[:, to : to + 16, :] = jnp.concatenate(parts, axis=1).astype(BF16)
    for zh in range(4):
        piece = g_ref[zh, 512:528, :].astype(F32)
        for b in range(8):
            sf_ref[b * 8 + zh * 2 : b * 8 + zh * 2 + 2, :] = piece[2 * b : 2 * b + 2, :]
    site = sf_ref[...].astype(BF16)
    coef = c_ref[...].astype(F32)
    coef = jnp.concatenate([coef, jnp.zeros((SITE_AT - COEF_AT - c_ref.shape[0], 128), F32)], axis=0).astype(BF16)
    for d in range(planes):
        out_ref[d, COEF_AT:SITE_AT, :] = coef
        out_ref[d, SITE_AT:, :] = site


def mix(half, a_ref, out_ref, gf_ref, cf_ref):
    planes, rows = out_ref.shape[:2]
    ops = rows // 8
    coef = a_ref[:, COEF_AT : COEF_AT + ops, :].astype(F32).reshape(planes * ops, 128).astype(BF16)
    gf_ref[...] = a_ref[:, half * 64 : half * 64 + 64, :].astype(F32).reshape(1024, 128)
    for r in range(8):
        block = gf_ref[pl.ds(r, 128, stride=8), :].astype(BF16)
        cf_ref[pl.ds(r, planes * ops, stride=8), :] = jnp.dot(coef, block, preferred_element_type=F32)

    def finish(d, _):
        at = pl.multiple_of(d * rows, 16)
        out_ref[d] = cf_ref[pl.ds(at, rows), :].astype(BF16)
        return 0

    lax.fori_loop(0, planes, finish, 0, unroll=4)


def mix_one(*refs):
    mix(0, *refs)


def mix_zero(*refs):
    mix(1, *refs)


def state_order(coupling_ref):
    c = [coupling_ref[0, t] for t in range(4)]
    zero, two, low, high = (jnp.int32(0) for _ in range(4))
    for t in range(4):
        zero = jnp.where(c[t] == 0, t, zero)
        two = jnp.where(c[t] == 2, t, two)
        high = jnp.where(c[t] == 1, t, high)
    for t in reversed(range(4)):
        low = jnp.where(c[t] == 1, t, low)
    return [zero, low, high, two]


def site_kernel(coupling_ref, size_ref, a_ref, own_ref):
    first = 4 * lax.axis_index("zl") + 2 * lax.axis_index("core")
    line = lax.broadcasted_iota(jnp.int32, (128, 128), 0)
    order = state_order(coupling_ref)
    for n in range(4):
        at = pl.multiple_of(SITE_AT + order[n] * 16, 16)
        both = a_ref[:, pl.ds(at, 16), :].astype(F32)
        for s in range(2):
            block = both[:, s * 8 : (s + 1) * 8, :].reshape(128, 128)
            block = jnp.where(line < size_ref[first + s], block, 0.0)
            own_ref[s, :, n * 128 : (n + 1) * 128] = block.astype(BF16)


def combine(r_ref, own, h):
    both = r_ref[:, pl.ds(pl.multiple_of(h * 16, 16), 16), :].astype(F32)
    pair = []
    for e in range(2):
        summed = both[:, e * 8 : (e + 1) * 8, :].reshape(128, 128)
        pair.append((own[e].astype(F32) + summed).astype(BF16))
    return pair


def inner(block, right):
    return jnp.dot(block, right, preferred_element_type=F32).astype(BF16)


def joined(parts, first, last):
    return jnp.concatenate([v[:, first:last] for v in parts], axis=1)


def stacked(parts, first):
    tall = [jnp.concatenate([v[:, first : first + 128], v[:, first + 128 : first + 256]], axis=0) for v in parts]
    return jnp.concatenate(tall, axis=1)


def product(left, right):
    return jnp.dot(left, right, preferred_element_type=F32)


def turned(pool_ref, s, states):
    blocks = [pool_ref[s, :, n * 128 : (n + 1) * 128].astype(F32).T for n in states]
    return jnp.concatenate(blocks, axis=1).astype(BF16)


def pool_kernel(own_ref, up_ref, pool_ref, early_ref, last_ref):
    for s in range(2):
        pool_ref[s] = own_ref[s]
        pool_ref[2 + s] = up_ref[s]
        early_ref[1 + s] = up_ref[s, :, 384:]
        last_ref[s] = own_ref[s, :, 384:]
    early_ref[0] = own_ref[1, :, 384:]
    early_ref[3] = turned(own_ref, 1, (3,))
    last_ref[2] = up_ref[0, :, 384:]
    last_ref[3] = turned(own_ref, 0, (3,))


def front_kernel(charge_ref, r_ref, op_ref, early_ref, out_ref, comb_ref):
    def step(h, _):
        pair = combine(r_ref, [op_ref[2 * h + e] for e in range(2)], h)
        parts = []
        for e in range(2):
            comb_ref[2 * h + e] = pair[e]
            parts.append(inner(pair[e], early_ref[charge_ref[2 * h + e]]))
        two = product(early_ref[3], joined(parts, 0, 128))
        for e in range(2):
            out_ref[2 * h + e] = two[:, e * 128 : (e + 1) * 128].astype(BF16)
        return 0

    lax.fori_loop(0, op_ref.shape[0] // 2, step, 0, unroll=12)


def middle_kernel(charge_ref, comb_ref, pool_ref, next_ref, again_ref, left_ref):
    again_ref[...] = pool_ref[...]
    left_ref[...] = turned(pool_ref, 1, (1, 2))

    def step(h, _):
        parts = [inner(comb_ref[2 * h + e], pool_ref[charge_ref[2 * h + e] + 1, :, 128:384]) for e in range(2)]
        one = product(left_ref[...], stacked(parts, 0))
        for e in range(2):
            next_ref[2 * h + e] = one[:, e * 128 : (e + 1) * 128]
        return 0

    lax.fori_loop(0, comb_ref.shape[0] // 2, step, 0, unroll=6)


def last_kernel(charge_ref, r_ref, op_ref, next_ref, last_ref, out_ref, comb_ref):
    def step(h, _):
        pair = combine(r_ref, [op_ref[2 * h + e] for e in range(2)], h)
        parts = []
        for e in range(2):
            comb_ref[2 * h + e] = pair[e]
            parts.append(inner(pair[e], last_ref[charge_ref[2 * h + e]]))
        two = product(last_ref[3], joined(parts, 0, 128))
        for e in range(2):
            k = 2 * h + e
            out_ref[k] = (two[:, e * 128 : (e + 1) * 128] + next_ref[k]).astype(BF16)
        return 0

    lax.fori_loop(0, op_ref.shape[0] // 2, step, 0, unroll=12)


def own_kernel(charge_ref, one_ref, zero_ref, pool_ref, first_ref, second_ref, left_ref):
    left_ref[...] = jnp.concatenate([turned(pool_ref, 0, (0, 1, 2)), turned(pool_ref, 1, (0,))], axis=1)

    def step(h, _):
        low, high = [], []
        for e in range(2):
            k = 2 * h + e
            q = charge_ref[k]
            low.append(inner(zero_ref[k], pool_ref[q, :, :384]))
            high.append(inner(one_ref[k], pool_ref[q + 1, :, :128]))
        first = product(left_ref[:, :128], joined(low, 0, 128))
        second = product(left_ref[:, 128:384], stacked(low, 128)) + product(left_ref[:, 384:], joined(high, 0, 128))
        for e in range(2):
            k, at = 2 * h + e, slice(e * 128, (e + 1) * 128)
            first_ref[k] = first[:, at]
            second_ref[k] = second[:, at]
        return 0

    lax.fori_loop(0, one_ref.shape[0] // 2, step, 0, unroll=2)


def close(sector, kept_ref, came_ref, out_hbm, done_ref, sems):
    size = kept_ref.shape[0] // 3
    moves = []
    for piece in range(3):
        at = slice(piece * size, (piece + 1) * size)
        done_ref[at] = (kept_ref[at] + came_ref[at].astype(F32)).astype(BF16)
        moves.append(pltpu.make_async_copy(done_ref.at[at], out_hbm.at[at, sector], sems.at[piece]))
        moves[-1].start()
    for move in moves:
        move.wait()


def close_one(kept_ref, came_ref, out_hbm, done_ref, sems):
    close(1, kept_ref, came_ref, out_hbm, done_ref, sems)


def close_zero(kept_ref, came_ref, _, out_hbm, done_ref, sems):
    close(0, kept_ref, came_ref, out_hbm, done_ref, sems)


def body(site_tensor, operators, one_index, weights, comp_charge, one_charge, sector_size, coupling):
    ops = operators.shape[0]
    sds = jax.ShapeDtypeStruct
    column = jnp.concatenate([one_index.reshape(512, 128), site_tensor.reshape(16, 128)], axis=0)
    far = lax.all_gather(column, "zh", axis=0)
    coef = jnp.where(comp_charge[:, None] == one_charge[None, :], weights, jnp.zeros((), BF16))
    message = call(
        spread_kernel, sds((16, MESSAGE, 128), BF16), [VMEM, VMEM], VMEM, [pltpu.VMEM((64, 128), F32)]
    )(coef, far)
    near = lax.all_to_all(message, PLANE, 0, 0, tiled=True)
    rows = ops * 8
    mixed = sds((16, rows, 128), BF16)
    scratch = [pltpu.VMEM((1024, 128), F32), pltpu.VMEM((16 * rows, 128), F32)]
    flops = 2 * ops * 2 * 128**3
    half, wide, site = sds((ops, 128, 128), BF16), sds((ops, 128, 128), F32), sds((2, 128, 512), BF16)
    mixed_one = call(mix_one, mixed, [VMEM], VMEM, scratch)(near)
    landed_one = lax.all_to_all(mixed_one, PLANE, 0, 0, tiled=True)
    own = call(site_kernel, site, [SMEM, SMEM, VMEM], VMEM)(coupling, sector_size, near)
    mixed_zero = call(mix_zero, mixed, [VMEM], VMEM, scratch)(near)
    zero, one = operators[:, 0], operators[:, 1]
    landed_zero = lax.all_to_all(mixed_zero, PLANE, 0, 0, tiled=True)
    upper = shift(own, -1)
    few = sds((4, 128, 128), BF16)
    pool, early, last = call(pool_kernel, [sds((4, 128, 512), BF16), few, few], [VMEM] * 2, [VMEM] * 3)(own, upper)
    leave, comb_one = call(front_kernel, [half, half], [SMEM] + [VMEM] * 3, [VMEM] * 2, flops=flops)(
        comp_charge, landed_one, one, early
    )
    came_one = shift(leave, 1)
    toward, again = call(
        middle_kernel,
        [wide, sds((4, 128, 512), BF16)],
        [SMEM] + [VMEM] * 2,
        [VMEM] * 2,
        [pltpu.VMEM((128, 256), BF16)],
        flops=2 * flops,
    )(comp_charge, comb_one, pool)
    leave, comb_zero = call(last_kernel, [half, half], [SMEM] + [VMEM] * 4, [VMEM] * 2, flops=flops)(
        comp_charge, landed_zero, zero, toward, last
    )
    came_zero = shift(leave, 1)
    first, second = call(
        own_kernel, [wide, wide], [SMEM] + [VMEM] * 3, [VMEM] * 2, [pltpu.VMEM((128, 512), BF16)], flops=4 * flops
    )(comp_charge, comb_one, comb_zero, again)
    whole = sds((ops, 2, 128, 128), BF16)
    scratch = [pltpu.VMEM((ops, 128, 128), BF16), DMA((3,))]
    out = call(close_one, whole, [VMEM] * 2, HBM, scratch)(second, came_one)
    return call(close_zero, whole, [VMEM, VMEM, HBM], HBM, scratch, input_output_aliases={2: 0})(first, came_zero, out)


def solution(mesh):
    fine = Mesh(mesh.devices.reshape(4, 4, 4, 4, 2), ("x", "y", "zh", "zl", "core"))
    pair, sector = ("x", "y", "zh"), ("zl", "core")
    return jax.shard_map(
        body,
        mesh=fine,
        in_specs=(
            P(None, sector, pair, None),
            P(pair, sector, None, None),
            P(pair, sector, None, None),
            P(pair, None),
            P(pair),
            P(),
            P(),
            P(),
        ),
        out_specs=P(pair, sector, None, None),
        check_vma=False,
    )
```

```python
import jax
import jax.numpy as jnp
from jax import lax
from jax.experimental import pallas as pl
from jax.experimental.pallas import tpu as pltpu
from jax.sharding import Mesh, PartitionSpec as P

F32 = jnp.float32
BF16 = jnp.bfloat16
PLANE = ("x", "y")
GROUP = ("zl", "core")
VMEM = pl.BlockSpec(memory_space=pltpu.VMEM)
SMEM = pl.BlockSpec(memory_space=pltpu.SMEM)
HBM = pl.BlockSpec(memory_space=pltpu.MemorySpace.HBM)
DMA = pltpu.SemaphoreType.DMA
COEF_AT, SITE_AT, MESSAGE = 128, 160, 224


def call(body, out, ins, outs, scratch=(), flops=0, moved=4 << 20, grant=16 << 20, **more):
    return pl.pallas_call(
        body,
        out_shape=out,
        in_specs=ins,
        out_specs=outs,
        scratch_shapes=list(scratch),
        cost_estimate=pl.CostEstimate(flops=flops, bytes_accessed=moved, transcendentals=0),
        compiler_params=pltpu.CompilerParams(vmem_limit_bytes=grant),
        **more,
    )


def shift(value, steps):
    count = lax.axis_size(GROUP)
    first, last = max(0, -steps), min(count, count - steps)
    return lax.ppermute(value, GROUP, [(a, a + steps) for a in range(first, last)])


def spread_kernel(c_ref, g_ref, out_ref, sf_ref):
    planes = out_ref.shape[0]
    for half in range(2):
        for zh in range(4):
            parts = []
            for j in range(2):
                at = (j * 2 + 1 - half) * 128
                parts.append(g_ref[zh, at : at + 128, :].astype(F32).reshape(planes, 8, 128))
            to = half * 64 + zh * 16
            out_ref[:, to : to + 16, :] = jnp.concatenate(parts, axis=1).astype(BF16)
    for zh in range(4):
        piece = g_ref[zh, 512:528, :].astype(F32)
        for b in range(8):
            sf_ref[b * 8 + zh * 2 : b * 8 + zh * 2 + 2, :] = piece[2 * b : 2 * b + 2, :]
    site = sf_ref[...].astype(BF16)
    coef = c_ref[...].astype(F32)
    coef = jnp.concatenate([coef, jnp.zeros((SITE_AT - COEF_AT - c_ref.shape[0], 128), F32)], axis=0).astype(BF16)
    for d in range(planes):
        out_ref[d, COEF_AT:SITE_AT, :] = coef
        out_ref[d, SITE_AT:, :] = site


def mix_kernel(a_ref, out_hbm, gf_ref, cf_ref, out_ref, sems):
    planes, rows = out_ref.shape[0], out_ref.shape[1] // 2
    ops = rows // 8
    coef = a_ref[:, COEF_AT : COEF_AT + ops, :].astype(F32).reshape(planes * ops, 128).astype(BF16)
    moves = []
    for half in range(2):
        gf_ref[half] = a_ref[:, half * 64 : half * 64 + 64, :].astype(F32).reshape(1024, 128)
        for r in range(8):
            block = gf_ref[half, pl.ds(r, 128, stride=8), :].astype(BF16)
            cf_ref[half, pl.ds(r, planes * ops, stride=8), :] = jnp.dot(coef, block, preferred_element_type=F32)

        def finish(d, _, half=half):
            at = pl.multiple_of(d * rows, 16)
            out_ref[d, half * rows : (half + 1) * rows, :] = cf_ref[half, pl.ds(at, rows), :].astype(BF16)
            return 0

        lax.fori_loop(0, planes, finish, 0, unroll=4)
        at = slice(half * rows, (half + 1) * rows)
        moves.append(pltpu.make_async_copy(out_ref.at[:, at], out_hbm.at[:, at], sems.at[half]))
        moves[-1].start()
    for move in moves:
        move.wait()


def state_order(coupling_ref):
    c = [coupling_ref[0, t] for t in range(4)]
    zero, two, low, high = (jnp.int32(0) for _ in range(4))
    for t in range(4):
        zero = jnp.where(c[t] == 0, t, zero)
        two = jnp.where(c[t] == 2, t, two)
        high = jnp.where(c[t] == 1, t, high)
    for t in reversed(range(4)):
        low = jnp.where(c[t] == 1, t, low)
    return [zero, low, high, two]


def site_kernel(coupling_ref, size_ref, a_ref, own_ref):
    first = 4 * lax.axis_index("zl") + 2 * lax.axis_index("core")
    line = lax.broadcasted_iota(jnp.int32, (128, 128), 0)
    order = state_order(coupling_ref)
    for n in range(4):
        at = pl.multiple_of(SITE_AT + order[n] * 16, 16)
        both = a_ref[:, pl.ds(at, 16), :].astype(F32)
        for s in range(2):
            block = both[:, s * 8 : (s + 1) * 8, :].reshape(128, 128)
            block = jnp.where(line < size_ref[first + s], block, 0.0)
            own_ref[s, :, n * 128 : (n + 1) * 128] = block.astype(BF16)


def combine(r_ref, op_ref, h, sector):
    base = (1 - sector) * (r_ref.shape[1] // 2)
    both = r_ref[:, pl.ds(pl.multiple_of(base + h * 16, 16), 16), :].astype(F32)
    pair = []
    for e in range(2):
        summed = both[:, e * 8 : (e + 1) * 8, :].reshape(128, 128)
        pair.append((op_ref[2 * h + e].astype(F32) + summed).astype(BF16))
    return pair


def inner(block, right):
    return jnp.dot(block, right, preferred_element_type=F32).astype(BF16)


def joined(parts, first, last):
    return jnp.concatenate([v[:, first:last] for v in parts], axis=1)


def stacked(parts, first):
    tall = [jnp.concatenate([v[:, first : first + 128], v[:, first + 128 : first + 256]], axis=0) for v in parts]
    return jnp.concatenate(tall, axis=1)


def product(left, right):
    return jnp.dot(left, right, preferred_element_type=F32)


def turned(pool_ref, s, states):
    blocks = [pool_ref[s, :, n * 128 : (n + 1) * 128].astype(F32).T for n in states]
    return jnp.concatenate(blocks, axis=1).astype(BF16)


def pool_kernel(own_ref, up_ref, pool_ref, early_ref):
    for s in range(2):
        pool_ref[s] = own_ref[s]
        pool_ref[2 + s] = up_ref[s]
        early_ref[1 + s] = up_ref[s, :, 384:]
    early_ref[0] = own_ref[1, :, 384:]
    early_ref[3] = turned(own_ref, 1, (3,))


def front_kernel(charge_ref, r_ref, op_ref, early_ref, out_ref, comb_ref):
    def step(h, _):
        pair = combine(r_ref, op_ref, h, 1)
        parts = []
        for e in range(2):
            comb_ref[2 * h + e] = pair[e]
            parts.append(inner(pair[e], early_ref[charge_ref[2 * h + e]]))
        two = product(early_ref[3], joined(parts, 0, 128))
        for e in range(2):
            out_ref[2 * h + e] = two[:, e * 128 : (e + 1) * 128].astype(BF16)
        return 0

    lax.fori_loop(0, op_ref.shape[0] // 2, step, 0, unroll=12)


def last_kernel(charge_ref, r_ref, op_ref, one_ref, pool_ref, out_ref, comb_ref, left_ref):
    left_ref[...] = jnp.concatenate([turned(pool_ref, 1, (1, 2)), turned(pool_ref, 0, (3,))], axis=1)

    def step(h, _):
        pair = combine(r_ref, op_ref, h, 0)
        tall = []
        for e in range(2):
            k = 2 * h + e
            q = charge_ref[k]
            comb_ref[k] = pair[e]
            ones = inner(one_ref[k], pool_ref[q + 1, :, 128:384])
            two = inner(pair[e], pool_ref[q, :, 384:])
            tall.append(jnp.concatenate([ones[:, :128], ones[:, 128:], two], axis=0))
        total = product(left_ref[...], jnp.concatenate(tall, axis=1))
        for e in range(2):
            out_ref[2 * h + e] = total[:, e * 128 : (e + 1) * 128].astype(BF16)
        return 0

    lax.fori_loop(0, one_ref.shape[0] // 2, step, 0, unroll=6)


def own_kernel(charge_ref, one_ref, zero_ref, pool_ref, first_ref, second_ref, left_ref):
    left_ref[...] = jnp.concatenate([turned(pool_ref, 0, (0, 1, 2)), turned(pool_ref, 1, (0,))], axis=1)

    def step(h, _):
        low, high = [], []
        for e in range(2):
            k = 2 * h + e
            q = charge_ref[k]
            low.append(inner(zero_ref[k], pool_ref[q, :, :384]))
            high.append(inner(one_ref[k], pool_ref[q + 1, :, :128]))
        first = product(left_ref[:, :128], joined(low, 0, 128))
        second = product(left_ref[:, 128:384], stacked(low, 128)) + product(left_ref[:, 384:], joined(high, 0, 128))
        for e in range(2):
            k, at = 2 * h + e, slice(e * 128, (e + 1) * 128)
            first_ref[k] = first[:, at]
            second_ref[k] = second[:, at]
        return 0

    lax.fori_loop(0, one_ref.shape[0] // 2, step, 0, unroll=2)


def close(sector, kept_ref, came_ref, out_hbm, done_ref, sems):
    size = kept_ref.shape[0] // 3
    moves = []
    for piece in range(3):
        at = slice(piece * size, (piece + 1) * size)
        done_ref[at] = (kept_ref[at] + came_ref[at].astype(F32)).astype(BF16)
        moves.append(pltpu.make_async_copy(done_ref.at[at], out_hbm.at[at, sector], sems.at[piece]))
        moves[-1].start()
    for move in moves:
        move.wait()


def close_one(kept_ref, came_ref, out_hbm, done_ref, sems):
    close(1, kept_ref, came_ref, out_hbm, done_ref, sems)


def close_zero(kept_ref, came_ref, _, out_hbm, done_ref, sems):
    close(0, kept_ref, came_ref, out_hbm, done_ref, sems)


def body(site_tensor, operators, one_index, weights, comp_charge, one_charge, sector_size, coupling):
    ops = operators.shape[0]
    sds = jax.ShapeDtypeStruct
    column = jnp.concatenate([one_index.reshape(512, 128), site_tensor.reshape(16, 128)], axis=0)
    far = lax.all_gather(column, "zh", axis=0)
    coef = jnp.where(comp_charge[:, None] == one_charge[None, :], weights, jnp.zeros((), BF16))
    message = call(
        spread_kernel, sds((16, MESSAGE, 128), BF16), [VMEM, VMEM], VMEM, [pltpu.VMEM((64, 128), F32)]
    )(coef, far)
    near = lax.all_to_all(message, PLANE, 0, 0, tiled=True)
    rows = ops * 8
    scratch = [pltpu.VMEM((2, 1024, 128), F32), pltpu.VMEM((2, 16 * rows, 128), F32)]
    flops = 2 * ops * 2 * 128**3
    half, wide, site = sds((ops, 128, 128), BF16), sds((ops, 128, 128), F32), sds((2, 128, 512), BF16)
    mixed = call(
        mix_kernel,
        pltpu.HBM((16, 2 * rows, 128), BF16),
        [VMEM],
        HBM,
        scratch + [pltpu.VMEM((16, 2 * rows, 128), BF16), DMA((2,))],
    )(near)
    landed = lax.all_to_all(mixed, PLANE, 0, 0, tiled=True)
    own = call(site_kernel, site, [SMEM, SMEM, VMEM], VMEM)(coupling, sector_size, near)
    upper = shift(own, -1)
    pool, early = call(
        pool_kernel, [sds((4, 128, 512), BF16), sds((4, 128, 128), BF16)], [VMEM] * 2, [VMEM] * 2
    )(own, upper)
    zero, one = operators[:, 0], operators[:, 1]
    leave, comb_one = call(front_kernel, [half, half], [SMEM] + [VMEM] * 3, [VMEM] * 2, flops=flops)(
        comp_charge, landed, one, early
    )
    came_one = shift(leave, 1)
    leave, comb_zero = call(
        last_kernel, [half, half], [SMEM] + [VMEM] * 4, [VMEM] * 2, [pltpu.VMEM((128, 384), BF16)], flops=3 * flops
    )(comp_charge, landed, zero, comb_one, pool)
    came_zero = shift(leave, 1)
    first, second = call(
        own_kernel, [wide, wide], [SMEM] + [VMEM] * 3, [VMEM] * 2, [pltpu.VMEM((128, 512), BF16)], flops=4 * flops
    )(comp_charge, comb_one, comb_zero, pool)
    whole = sds((ops, 2, 128, 128), BF16)
    scratch = [pltpu.VMEM((ops, 128, 128), BF16), DMA((3,))]
    out = call(close_one, whole, [VMEM] * 2, HBM, scratch)(second, came_one)
    return call(close_zero, whole, [VMEM, VMEM, HBM], HBM, scratch, input_output_aliases={2: 0})(first, came_zero, out)


def solution(mesh):
    fine = Mesh(mesh.devices.reshape(4, 4, 4, 4, 2), ("x", "y", "zh", "zl", "core"))
    pair, sector = ("x", "y", "zh"), ("zl", "core")
    return jax.shard_map(
        body,
        mesh=fine,
        in_specs=(
            P(None, sector, pair, None),
            P(pair, sector, None, None),
            P(pair, sector, None, None),
            P(pair, None),
            P(pair),
            P(),
            P(),
            P(),
        ),
        out_specs=P(pair, sector, None, None),
        check_vma=False,
    )
```

```python
import jax
import jax.numpy as jnp
from jax import lax
from jax.experimental import pallas as pl
from jax.experimental.pallas import tpu as pltpu
from jax.sharding import Mesh, PartitionSpec as P

F32 = jnp.float32
BF16 = jnp.bfloat16
PLANE = ("x", "y")
GROUP = ("zl", "core")
VMEM = pl.BlockSpec(memory_space=pltpu.VMEM)
SMEM = pl.BlockSpec(memory_space=pltpu.SMEM)
HBM = pl.BlockSpec(memory_space=pltpu.MemorySpace.HBM)
DMA = pltpu.SemaphoreType.DMA
SITE_AT, COEF_AT = 128, 192


def call(body, out, ins, outs, scratch=(), flops=0, moved=4 << 20, grant=16 << 20, **more):
    return pl.pallas_call(
        body,
        out_shape=out,
        in_specs=ins,
        out_specs=outs,
        scratch_shapes=list(scratch),
        cost_estimate=pl.CostEstimate(flops=flops, bytes_accessed=moved, transcendentals=0),
        compiler_params=pltpu.CompilerParams(vmem_limit_bytes=grant),
        **more,
    )


def shift(value, steps):
    count = lax.axis_size(GROUP)
    first, last = max(0, -steps), min(count, count - steps)
    return lax.ppermute(value, GROUP, [(a, a + steps) for a in range(first, last)])


def spread_kernel(c_ref, g_ref, out_ref, sf_ref):
    planes = out_ref.shape[0]
    for half in range(2):
        for zh in range(4):
            parts = []
            for j in range(2):
                at = (j * 2 + 1 - half) * 128
                parts.append(g_ref[zh, at : at + 128, :].astype(F32).reshape(planes, 8, 128))
            to = half * 64 + zh * 16
            out_ref[:, to : to + 16, :] = jnp.concatenate(parts, axis=1).astype(BF16)
    for zh in range(4):
        piece = g_ref[zh, 512:528, :].astype(F32)
        for b in range(8):
            sf_ref[b * 8 + zh * 2 : b * 8 + zh * 2 + 2, :] = piece[2 * b : 2 * b + 2, :]
    site = sf_ref[...].astype(BF16)
    for d in range(planes):
        out_ref[d, SITE_AT:COEF_AT, :] = site
        out_ref[d, COEF_AT:, :] = c_ref[...]


def mix_kernel(a_ref, out_hbm, gf_ref, cf_ref, out_ref, sems):
    planes, rows = out_ref.shape[0], out_ref.shape[1] // 2
    ops = rows // 8
    coef = a_ref[:, COEF_AT : COEF_AT + ops, :].astype(F32).reshape(planes * ops, 128).astype(BF16)
    moves = []
    for half in range(2):
        gf_ref[half] = a_ref[:, half * 64 : half * 64 + 64, :].astype(F32).reshape(1024, 128)
        for r in range(8):
            block = gf_ref[half, pl.ds(r, 128, stride=8), :].astype(BF16)
            cf_ref[half, pl.ds(r, planes * ops, stride=8), :] = jnp.dot(coef, block, preferred_element_type=F32)

        def finish(d, _, half=half):
            at = pl.multiple_of(d * rows, 16)
            out_ref[d, half * rows : (half + 1) * rows, :] = cf_ref[half, pl.ds(at, rows), :].astype(BF16)
            return 0

        lax.fori_loop(0, planes, finish, 0, unroll=4)
        at = slice(half * rows, (half + 1) * rows)
        moves.append(pltpu.make_async_copy(out_ref.at[:, at], out_hbm.at[:, at], sems.at[half]))
        moves[-1].start()
    for move in moves:
        move.wait()


def state_order(coupling_ref):
    c = [coupling_ref[0, t] for t in range(4)]
    zero, two, low, high = (jnp.int32(0) for _ in range(4))
    for t in range(4):
        zero = jnp.where(c[t] == 0, t, zero)
        two = jnp.where(c[t] == 2, t, two)
        high = jnp.where(c[t] == 1, t, high)
    for t in reversed(range(4)):
        low = jnp.where(c[t] == 1, t, low)
    return [zero, low, high, two]


def site_kernel(coupling_ref, size_ref, a_ref, own_ref):
    first = 4 * lax.axis_index("zl") + 2 * lax.axis_index("core")
    line = lax.broadcasted_iota(jnp.int32, (128, 128), 0)
    order = state_order(coupling_ref)
    for n in range(4):
        at = pl.multiple_of(SITE_AT + order[n] * 16, 16)
        both = a_ref[:, pl.ds(at, 16), :].astype(F32)
        for s in range(2):
            block = both[:, s * 8 : (s + 1) * 8, :].reshape(128, 128)
            block = jnp.where(line < size_ref[first + s], block, 0.0)
            own_ref[s, :, n * 128 : (n + 1) * 128] = block.astype(BF16)


def combine(r_ref, op_ref, h, sector):
    base = (1 - sector) * (r_ref.shape[1] // 2)
    both = r_ref[:, pl.ds(pl.multiple_of(base + h * 16, 16), 16), :].astype(F32)
    pair = []
    for e in range(2):
        summed = both[:, e * 8 : (e + 1) * 8, :].reshape(128, 128)
        pair.append((op_ref[2 * h + e].astype(F32) + summed).astype(BF16))
    return pair


def inner(block, right):
    return jnp.dot(block, right, preferred_element_type=F32).astype(BF16)


def joined(parts, first, last):
    return jnp.concatenate([v[:, first:last] for v in parts], axis=1)


def stacked(parts, first):
    tall = [jnp.concatenate([v[:, first : first + 128], v[:, first + 128 : first + 256]], axis=0) for v in parts]
    return jnp.concatenate(tall, axis=1)


def product(left, right):
    return jnp.dot(left, right, preferred_element_type=F32)


def turned(pool_ref, s, states):
    blocks = [pool_ref[s, :, n * 128 : (n + 1) * 128].astype(F32).T for n in states]
    return jnp.concatenate(blocks, axis=1).astype(BF16)


def pool_kernel(own_ref, up_ref, pool_ref, early_ref):
    for s in range(2):
        pool_ref[s] = own_ref[s]
        pool_ref[2 + s] = up_ref[s]
        early_ref[1 + s] = up_ref[s, :, 384:]
    early_ref[0] = own_ref[1, :, 384:]
    early_ref[3] = turned(own_ref, 1, (3,))


def front_kernel(core, charge_ref, r_ref, op_ref, early_ref, out_ref):
    @pl.when(lax.axis_index("core") == core)
    def _():
        def step(h, _):
            pair = combine(r_ref, op_ref, h, 1)
            parts = [inner(pair[e], early_ref[charge_ref[2 * h + e]]) for e in range(2)]
            two = product(early_ref[3], joined(parts, 0, 128))
            for e in range(2):
                out_ref[2 * h + e] = two[:, e * 128 : (e + 1) * 128].astype(BF16)
            return 0

        lax.fori_loop(0, op_ref.shape[0] // 2, step, 0, unroll=12)


def front_far(*refs):
    front_kernel(1, *refs)


def front_near(*refs):
    front_kernel(0, *refs)


def last_kernel(charge_ref, r_ref, zero_ref, one_ref, pool_ref, out_ref, comb_ref, other_ref, left_ref):
    left_ref[...] = jnp.concatenate([turned(pool_ref, 1, (1, 2)), turned(pool_ref, 0, (3,))], axis=1)

    def step(h, _):
        pair = combine(r_ref, zero_ref, h, 0)
        high = combine(r_ref, one_ref, h, 1)
        tall = []
        for e in range(2):
            k = 2 * h + e
            q = charge_ref[k]
            comb_ref[k], other_ref[k] = pair[e], high[e]
            ones = inner(high[e], pool_ref[q + 1, :, 128:384])
            two = inner(pair[e], pool_ref[q, :, 384:])
            tall.append(jnp.concatenate([ones[:, :128], ones[:, 128:], two], axis=0))
        total = product(left_ref[...], jnp.concatenate(tall, axis=1))
        for e in range(2):
            out_ref[2 * h + e] = total[:, e * 128 : (e + 1) * 128].astype(BF16)
        return 0

    lax.fori_loop(0, one_ref.shape[0] // 2, step, 0, unroll=6)


def own_kernel(charge_ref, one_ref, zero_ref, pool_ref, first_ref, second_ref, left_ref):
    left_ref[...] = jnp.concatenate([turned(pool_ref, 0, (0, 1, 2)), turned(pool_ref, 1, (0,))], axis=1)

    def step(h, _):
        low, high = [], []
        for e in range(2):
            k = 2 * h + e
            q = charge_ref[k]
            low.append(inner(zero_ref[k], pool_ref[q, :, :384]))
            high.append(inner(one_ref[k], pool_ref[q + 1, :, :128]))
        first = product(left_ref[:, :128], joined(low, 0, 128))
        second = product(left_ref[:, 128:384], stacked(low, 128)) + product(left_ref[:, 384:], joined(high, 0, 128))
        for e in range(2):
            k, at = 2 * h + e, slice(e * 128, (e + 1) * 128)
            first_ref[k] = first[:, at]
            second_ref[k] = second[:, at]
        return 0

    lax.fori_loop(0, one_ref.shape[0] // 2, step, 0, unroll=2)


def close(sector, kept_ref, came_refs, out_hbm, done_ref, sems):
    size = kept_ref.shape[0] // 3
    moves = []
    for piece in range(3):
        at = slice(piece * size, (piece + 1) * size)
        total = kept_ref[at]
        for ref in came_refs:
            total = total + ref[at].astype(F32)
        done_ref[at] = total.astype(BF16)
        moves.append(pltpu.make_async_copy(done_ref.at[at], out_hbm.at[at, sector], sems.at[piece]))
        moves[-1].start()
    for move in moves:
        move.wait()


def close_one(kept_ref, far_ref, near_ref, out_hbm, done_ref, sems):
    close(1, kept_ref, (far_ref, near_ref), out_hbm, done_ref, sems)


def close_zero(kept_ref, came_ref, _, out_hbm, done_ref, sems):
    close(0, kept_ref, (came_ref,), out_hbm, done_ref, sems)


def body(site_tensor, operators, one_index, weights, comp_charge, one_charge, sector_size, coupling):
    ops = operators.shape[0]
    sds = jax.ShapeDtypeStruct
    column = jnp.concatenate([one_index.reshape(512, 128), site_tensor.reshape(16, 128)], axis=0)
    far = lax.all_gather(column, "zh", axis=0)
    coef = jnp.where(comp_charge[:, None] == one_charge[None, :], weights, jnp.zeros((), BF16))
    message = call(
        spread_kernel, sds((16, COEF_AT + ops, 128), BF16), [VMEM, VMEM], VMEM, [pltpu.VMEM((64, 128), F32)]
    )(coef, far)
    near = lax.all_to_all(message, PLANE, 0, 0, tiled=True)
    rows = ops * 8
    scratch = [pltpu.VMEM((2, 1024, 128), F32), pltpu.VMEM((2, 16 * rows, 128), F32)]
    flops = 2 * ops * 2 * 128**3
    half, wide, site = sds((ops, 128, 128), BF16), sds((ops, 128, 128), F32), sds((2, 128, 512), BF16)
    mixed = call(
        mix_kernel,
        pltpu.HBM((16, 2 * rows, 128), BF16),
        [VMEM],
        HBM,
        scratch + [pltpu.VMEM((16, 2 * rows, 128), BF16), DMA((2,))],
    )(near)
    landed = lax.all_to_all(mixed, PLANE, 0, 0, tiled=True)
    own = call(site_kernel, site, [SMEM, SMEM, VMEM], VMEM)(coupling, sector_size, near)
    upper = shift(own, -1)
    pool, early = call(
        pool_kernel, [sds((4, 128, 512), BF16), sds((4, 128, 128), BF16)], [VMEM] * 2, [VMEM] * 2
    )(own, upper)
    zero, one = operators[:, 0], operators[:, 1]
    leave = call(front_far, half, [SMEM] + [VMEM] * 3, VMEM, flops=flops)(comp_charge, landed, one, early)
    came_far = lax.ppermute(leave, GROUP, [(1, 2), (3, 4), (5, 6)])
    leave = call(front_near, half, [SMEM] + [VMEM] * 3, VMEM, flops=flops)(comp_charge, landed, one, early)
    came_near = lax.ppermute(leave, GROUP, [(0, 1), (2, 3), (4, 5), (6, 7)])
    leave, comb_zero, comb_one = call(
        last_kernel, [half] * 3, [SMEM] + [VMEM] * 4, [VMEM] * 3, [pltpu.VMEM((128, 384), BF16)], flops=3 * flops
    )(comp_charge, landed, zero, one, pool)
    came_zero = shift(leave, 1)
    first, second = call(
        own_kernel, [wide, wide], [SMEM] + [VMEM] * 3, [VMEM] * 2, [pltpu.VMEM((128, 512), BF16)], flops=4 * flops
    )(comp_charge, comb_one, comb_zero, pool)
    whole = sds((ops, 2, 128, 128), BF16)
    scratch = [pltpu.VMEM((ops, 128, 128), BF16), DMA((3,))]
    out = call(close_one, whole, [VMEM] * 3, HBM, scratch)(second, came_far, came_near)
    return call(close_zero, whole, [VMEM, VMEM, HBM], HBM, scratch, input_output_aliases={2: 0})(first, came_zero, out)


def solution(mesh):
    fine = Mesh(mesh.devices.reshape(4, 4, 4, 4, 2), ("x", "y", "zh", "zl", "core"))
    pair, sector = ("x", "y", "zh"), ("zl", "core")
    return jax.shard_map(
        body,
        mesh=fine,
        in_specs=(
            P(None, sector, pair, None),
            P(pair, sector, None, None),
            P(pair, sector, None, None),
            P(pair, None),
            P(pair),
            P(),
            P(),
            P(),
        ),
        out_specs=P(pair, sector, None, None),
        check_vma=False,
    )
```

```python
import jax
import jax.numpy as jnp
from jax import lax
from jax.experimental import pallas as pl
from jax.experimental.pallas import tpu as pltpu
from jax.sharding import Mesh, PartitionSpec as P

F32 = jnp.float32
BF16 = jnp.bfloat16
PLANE = ("x", "y")
GROUP = ("zl", "core")
VMEM = pl.BlockSpec(memory_space=pltpu.VMEM)
SMEM = pl.BlockSpec(memory_space=pltpu.SMEM)
HBM = pl.BlockSpec(memory_space=pltpu.MemorySpace.HBM)
DMA = pltpu.SemaphoreType.DMA
SITE_AT, COEF_AT = 128, 192


def call(body, out, ins, outs, scratch=(), flops=0, moved=4 << 20, grant=16 << 20, **more):
    return pl.pallas_call(
        body,
        out_shape=out,
        in_specs=ins,
        out_specs=outs,
        scratch_shapes=list(scratch),
        cost_estimate=pl.CostEstimate(flops=flops, bytes_accessed=moved, transcendentals=0),
        compiler_params=pltpu.CompilerParams(vmem_limit_bytes=grant),
        **more,
    )


def shift(value, steps):
    count = lax.axis_size(GROUP)
    first, last = max(0, -steps), min(count, count - steps)
    return lax.ppermute(value, GROUP, [(a, a + steps) for a in range(first, last)])


def spread_kernel(c_ref, g_ref, out_ref, sf_ref):
    planes = out_ref.shape[0]
    for half in range(2):
        for zh in range(4):
            parts = []
            for j in range(2):
                at = (j * 2 + 1 - half) * 128
                parts.append(g_ref[zh, at : at + 128, :].astype(F32).reshape(planes, 8, 128))
            to = half * 64 + zh * 16
            out_ref[:, to : to + 16, :] = jnp.concatenate(parts, axis=1).astype(BF16)
    for zh in range(4):
        piece = g_ref[zh, 512:528, :].astype(F32)
        for b in range(8):
            sf_ref[b * 8 + zh * 2 : b * 8 + zh * 2 + 2, :] = piece[2 * b : 2 * b + 2, :]
    site = sf_ref[...].astype(BF16)
    for d in range(planes):
        out_ref[d, SITE_AT:COEF_AT, :] = site
        out_ref[d, COEF_AT:, :] = c_ref[...]


def mix_kernel(a_ref, out_hbm, gf_ref, cf_ref, out_ref, sems):
    planes, rows = out_ref.shape[0], out_ref.shape[1] // 2
    ops = rows // 8
    coef = a_ref[:, COEF_AT : COEF_AT + ops, :].astype(F32).reshape(planes * ops, 128).astype(BF16)
    moves = []
    for half in range(2):
        gf_ref[half] = a_ref[:, half * 64 : half * 64 + 64, :].astype(F32).reshape(1024, 128)
        for r in range(8):
            block = gf_ref[half, pl.ds(r, 128, stride=8), :].astype(BF16)
            cf_ref[half, pl.ds(r, planes * ops, stride=8), :] = jnp.dot(coef, block, preferred_element_type=F32)

        def finish(d, _, half=half):
            at = pl.multiple_of(d * rows, 16)
            out_ref[d, half * rows : (half + 1) * rows, :] = cf_ref[half, pl.ds(at, rows), :].astype(BF16)
            return 0

        lax.fori_loop(0, planes, finish, 0, unroll=4)
        at = slice(half * rows, (half + 1) * rows)
        moves.append(pltpu.make_async_copy(out_ref.at[:, at], out_hbm.at[:, at], sems.at[half]))
        moves[-1].start()
    for move in moves:
        move.wait()


def state_order(coupling_ref):
    c = [coupling_ref[0, t] for t in range(4)]
    zero, two, low, high = (jnp.int32(0) for _ in range(4))
    for t in range(4):
        zero = jnp.where(c[t] == 0, t, zero)
        two = jnp.where(c[t] == 2, t, two)
        high = jnp.where(c[t] == 1, t, high)
    for t in reversed(range(4)):
        low = jnp.where(c[t] == 1, t, low)
    return [zero, low, high, two]


def site_kernel(coupling_ref, size_ref, a_ref, own_ref):
    first = 4 * lax.axis_index("zl") + 2 * lax.axis_index("core")
    line = lax.broadcasted_iota(jnp.int32, (128, 128), 0)
    order = state_order(coupling_ref)
    for n in range(4):
        at = pl.multiple_of(SITE_AT + order[n] * 16, 16)
        both = a_ref[:, pl.ds(at, 16), :].astype(F32)
        for s in range(2):
            block = both[:, s * 8 : (s + 1) * 8, :].reshape(128, 128)
            block = jnp.where(line < size_ref[first + s], block, 0.0)
            own_ref[s, :, n * 128 : (n + 1) * 128] = block.astype(BF16)


def combine(r_ref, op_ref, h, sector):
    base = (1 - sector) * (r_ref.shape[1] // 2)
    both = r_ref[:, pl.ds(pl.multiple_of(base + h * 16, 16), 16), :].astype(F32)
    pair = []
    for e in range(2):
        summed = both[:, e * 8 : (e + 1) * 8, :].reshape(128, 128)
        pair.append((op_ref[2 * h + e].astype(F32) + summed).astype(BF16))
    return pair


def inner(block, right):
    return jnp.dot(block, right, preferred_element_type=F32).astype(BF16)


def joined(parts, first, last):
    return jnp.concatenate([v[:, first:last] for v in parts], axis=1)


def stacked(parts, first):
    tall = [jnp.concatenate([v[:, first : first + 128], v[:, first + 128 : first + 256]], axis=0) for v in parts]
    return jnp.concatenate(tall, axis=1)


def product(left, right):
    return jnp.dot(left, right, preferred_element_type=F32)


def turned(pool_ref, s, states):
    blocks = [pool_ref[s, :, n * 128 : (n + 1) * 128].astype(F32).T for n in states]
    return jnp.concatenate(blocks, axis=1).astype(BF16)


def pool_kernel(own_ref, up_ref, pool_ref, early_ref):
    for s in range(2):
        pool_ref[s] = own_ref[s]
        pool_ref[2 + s] = up_ref[s]
        early_ref[1 + s] = up_ref[s, :, 384:]
    early_ref[0] = own_ref[1, :, 384:]
    early_ref[3] = turned(own_ref, 1, (3,))


def front(charge_ref, r_ref, op_ref, early_ref, out_ref):
    def step(h, _):
        pair = combine(r_ref, op_ref, h, 1)
        parts = [inner(pair[e], early_ref[charge_ref[2 * h + e]]) for e in range(2)]
        two = product(early_ref[3], joined(parts, 0, 128))
        for e in range(2):
            out_ref[2 * h + e] = two[:, e * 128 : (e + 1) * 128].astype(BF16)
        return 0

    lax.fori_loop(0, op_ref.shape[0] // 2, step, 0, unroll=12)


def front_far(*refs):
    @pl.when(lax.axis_index("core") == 1)
    def _():
        front(*refs)


def front_near(charge_ref, r_ref, op_ref, early_ref, came_ref, out_ref):
    @pl.when(lax.axis_index("core") == 0)
    def _():
        front(charge_ref, r_ref, op_ref, early_ref, out_ref)

    @pl.when(lax.axis_index("core") == 1)
    def _():
        out_ref[...] = came_ref[...]


def pick_kernel(leave_ref, came_ref, out_ref):
    @pl.when(lax.axis_index("core") == 0)
    def _():
        out_ref[...] = leave_ref[...]

    @pl.when(lax.axis_index("core") == 1)
    def _():
        out_ref[...] = came_ref[...]


def last_kernel(charge_ref, r_ref, zero_ref, one_ref, pool_ref, out_ref, comb_ref, other_ref, left_ref):
    left_ref[...] = jnp.concatenate([turned(pool_ref, 1, (1, 2)), turned(pool_ref, 0, (3,))], axis=1)

    def step(h, _):
        pair = combine(r_ref, zero_ref, h, 0)
        high = combine(r_ref, one_ref, h, 1)
        tall = []
        for e in range(2):
            k = 2 * h + e
            q = charge_ref[k]
            comb_ref[k], other_ref[k] = pair[e], high[e]
            ones = inner(high[e], pool_ref[q + 1, :, 128:384])
            two = inner(pair[e], pool_ref[q, :, 384:])
            tall.append(jnp.concatenate([ones[:, :128], ones[:, 128:], two], axis=0))
        total = product(left_ref[...], jnp.concatenate(tall, axis=1))
        for e in range(2):
            out_ref[2 * h + e] = total[:, e * 128 : (e + 1) * 128].astype(BF16)
        return 0

    lax.fori_loop(0, one_ref.shape[0] // 2, step, 0, unroll=6)


def own_kernel(charge_ref, one_ref, zero_ref, pool_ref, first_ref, second_ref, left_ref):
    left_ref[...] = jnp.concatenate([turned(pool_ref, 0, (0, 1, 2)), turned(pool_ref, 1, (0,))], axis=1)

    def step(h, _):
        low, high = [], []
        for e in range(2):
            k = 2 * h + e
            q = charge_ref[k]
            low.append(inner(zero_ref[k], pool_ref[q, :, :384]))
            high.append(inner(one_ref[k], pool_ref[q + 1, :, :128]))
        first = product(left_ref[:, :128], joined(low, 0, 128))
        second = product(left_ref[:, 128:384], stacked(low, 128)) + product(left_ref[:, 384:], joined(high, 0, 128))
        for e in range(2):
            k, at = 2 * h + e, slice(e * 128, (e + 1) * 128)
            first_ref[k] = first[:, at]
            second_ref[k] = second[:, at]
        return 0

    lax.fori_loop(0, one_ref.shape[0] // 2, step, 0, unroll=2)


def close(sector, kept_ref, came_ref, out_hbm, done_ref, sems):
    size = kept_ref.shape[0] // 3
    moves = []
    for piece in range(3):
        at = slice(piece * size, (piece + 1) * size)
        done_ref[at] = (kept_ref[at] + came_ref[at].astype(F32)).astype(BF16)
        moves.append(pltpu.make_async_copy(done_ref.at[at], out_hbm.at[at, sector], sems.at[piece]))
        moves[-1].start()
    for move in moves:
        move.wait()


def close_one(kept_ref, came_ref, out_hbm, done_ref, sems):
    close(1, kept_ref, came_ref, out_hbm, done_ref, sems)


def close_zero(kept_ref, came_ref, _, out_hbm, done_ref, sems):
    close(0, kept_ref, came_ref, out_hbm, done_ref, sems)


def body(site_tensor, operators, one_index, weights, comp_charge, one_charge, sector_size, coupling):
    ops = operators.shape[0]
    sds = jax.ShapeDtypeStruct
    column = jnp.concatenate([one_index.reshape(512, 128), site_tensor.reshape(16, 128)], axis=0)
    far = lax.all_gather(column, "zh", axis=0)
    coef = jnp.where(comp_charge[:, None] == one_charge[None, :], weights, jnp.zeros((), BF16))
    message = call(
        spread_kernel, sds((16, COEF_AT + ops, 128), BF16), [VMEM, VMEM], VMEM, [pltpu.VMEM((64, 128), F32)]
    )(coef, far)
    near = lax.all_to_all(message, PLANE, 0, 0, tiled=True)
    rows = ops * 8
    scratch = [pltpu.VMEM((2, 1024, 128), F32), pltpu.VMEM((2, 16 * rows, 128), F32)]
    flops = 2 * ops * 2 * 128**3
    half, wide, site = sds((ops, 128, 128), BF16), sds((ops, 128, 128), F32), sds((2, 128, 512), BF16)
    mixed = call(
        mix_kernel,
        pltpu.HBM((16, 2 * rows, 128), BF16),
        [VMEM],
        HBM,
        scratch + [pltpu.VMEM((16, 2 * rows, 128), BF16), DMA((2,))],
    )(near)
    landed = lax.all_to_all(mixed, PLANE, 0, 0, tiled=True)
    own = call(site_kernel, site, [SMEM, SMEM, VMEM], VMEM)(coupling, sector_size, near)
    upper = shift(own, -1)
    pool, early = call(
        pool_kernel, [sds((4, 128, 512), BF16), sds((4, 128, 128), BF16)], [VMEM] * 2, [VMEM] * 2
    )(own, upper)
    zero, one = operators[:, 0], operators[:, 1]
    onward = [(1, 3), (3, 5), (5, 7)]
    swap = [(i, i ^ 1) for i in range(8)]
    ins = [SMEM] + [VMEM] * 3
    leave = call(front_far, half, ins, VMEM, flops=flops)(comp_charge, landed, one, early)
    came = lax.ppermute(leave, GROUP, onward)
    leave, comb_zero, comb_one = call(
        last_kernel, [half] * 3, [SMEM] + [VMEM] * 4, [VMEM] * 3, [pltpu.VMEM((128, 384), BF16)], flops=3 * flops
    )(comp_charge, landed, zero, one, pool)
    came_far = lax.ppermute(leave, GROUP, onward)
    near_one = call(front_near, half, ins + [VMEM], VMEM, flops=flops)(comp_charge, landed, one, early, came)
    came_one = lax.ppermute(near_one, GROUP, swap)
    first, second = call(
        own_kernel, [wide, wide], ins, [VMEM] * 2, [pltpu.VMEM((128, 512), BF16)], flops=4 * flops
    )(comp_charge, comb_one, comb_zero, pool)
    near_zero = call(pick_kernel, half, [VMEM] * 2, VMEM)(leave, came_far)
    came_zero = lax.ppermute(near_zero, GROUP, swap)
    whole = sds((ops, 2, 128, 128), BF16)
    scratch = [pltpu.VMEM((ops, 128, 128), BF16), DMA((3,))]
    out = call(close_one, whole, [VMEM] * 2, HBM, scratch)(second, came_one)
    return call(close_zero, whole, [VMEM, VMEM, HBM], HBM, scratch, input_output_aliases={2: 0})(first, came_zero, out)


def solution(mesh):
    fine = Mesh(mesh.devices.reshape(4, 4, 4, 4, 2), ("x", "y", "zh", "zl", "core"))
    pair, sector = ("x", "y", "zh"), ("zl", "core")
    return jax.shard_map(
        body,
        mesh=fine,
        in_specs=(
            P(None, sector, pair, None),
            P(pair, sector, None, None),
            P(pair, sector, None, None),
            P(pair, None),
            P(pair),
            P(),
            P(),
            P(),
        ),
        out_specs=P(pair, sector, None, None),
        check_vma=False,
    )
```

```python
import jax
import jax.numpy as jnp
from jax import lax
from jax.experimental import pallas as pl
from jax.experimental.pallas import tpu as pltpu
from jax.sharding import Mesh, PartitionSpec as P

F32 = jnp.float32
BF16 = jnp.bfloat16
PLANE = ("x", "y")
GROUP = ("zl", "core")
VMEM = pl.BlockSpec(memory_space=pltpu.VMEM)
SMEM = pl.BlockSpec(memory_space=pltpu.SMEM)
HBM = pl.BlockSpec(memory_space=pltpu.MemorySpace.HBM)
DMA = pltpu.SemaphoreType.DMA
SITE_AT, COEF_AT = 128, 192


def call(body, out, ins, outs, scratch=(), flops=0, moved=4 << 20, grant=16 << 20, **more):
    return pl.pallas_call(
        body,
        out_shape=out,
        in_specs=ins,
        out_specs=outs,
        scratch_shapes=list(scratch),
        cost_estimate=pl.CostEstimate(flops=flops, bytes_accessed=moved, transcendentals=0),
        compiler_params=pltpu.CompilerParams(vmem_limit_bytes=grant),
        **more,
    )


def shift(value, steps):
    count = lax.axis_size(GROUP)
    first, last = max(0, -steps), min(count, count - steps)
    return lax.ppermute(value, GROUP, [(a, a + steps) for a in range(first, last)])


def spread_kernel(c_ref, g_ref, out_ref, sf_ref):
    planes = out_ref.shape[0]
    for half in range(2):
        for zh in range(4):
            parts = []
            for j in range(2):
                at = (j * 2 + 1 - half) * 128
                parts.append(g_ref[zh, at : at + 128, :].astype(F32).reshape(planes, 8, 128))
            to = half * 64 + zh * 16
            out_ref[:, to : to + 16, :] = jnp.concatenate(parts, axis=1).astype(BF16)
    for zh in range(4):
        piece = g_ref[zh, 512:528, :].astype(F32)
        for b in range(8):
            sf_ref[b * 8 + zh * 2 : b * 8 + zh * 2 + 2, :] = piece[2 * b : 2 * b + 2, :]
    site = sf_ref[...].astype(BF16)
    for d in range(planes):
        out_ref[d, SITE_AT:COEF_AT, :] = site
        out_ref[d, COEF_AT:, :] = c_ref[...]


def mix_kernel(a_ref, out_hbm, gf_ref, cf_ref, out_ref, sems):
    planes, rows = out_ref.shape[0], out_ref.shape[1] // 2
    ops = rows // 8
    coef = a_ref[:, COEF_AT : COEF_AT + ops, :].astype(F32).reshape(planes * ops, 128).astype(BF16)
    moves = []
    for half in range(2):
        gf_ref[half] = a_ref[:, half * 64 : half * 64 + 64, :].astype(F32).reshape(1024, 128)
        for r in range(8):
            block = gf_ref[half, pl.ds(r, 128, stride=8), :].astype(BF16)
            cf_ref[half, pl.ds(r, planes * ops, stride=8), :] = jnp.dot(coef, block, preferred_element_type=F32)

        def finish(d, _, half=half):
            at = pl.multiple_of(d * rows, 16)
            out_ref[d, half * rows : (half + 1) * rows, :] = cf_ref[half, pl.ds(at, rows), :].astype(BF16)
            return 0

        lax.fori_loop(0, planes, finish, 0, unroll=4)
        at = slice(half * rows, (half + 1) * rows)
        moves.append(pltpu.make_async_copy(out_ref.at[:, at], out_hbm.at[:, at], sems.at[half]))
        moves[-1].start()
    for move in moves:
        move.wait()


def state_order(coupling_ref):
    c = [coupling_ref[0, t] for t in range(4)]
    zero, two, low, high = (jnp.int32(0) for _ in range(4))
    for t in range(4):
        zero = jnp.where(c[t] == 0, t, zero)
        two = jnp.where(c[t] == 2, t, two)
        high = jnp.where(c[t] == 1, t, high)
    for t in reversed(range(4)):
        low = jnp.where(c[t] == 1, t, low)
    return [zero, low, high, two]


def site_kernel(coupling_ref, size_ref, a_ref, own_ref):
    first = 4 * lax.axis_index("zl") + 2 * lax.axis_index("core")
    line = lax.broadcasted_iota(jnp.int32, (128, 128), 0)
    order = state_order(coupling_ref)
    for n in range(4):
        at = pl.multiple_of(SITE_AT + order[n] * 16, 16)
        both = a_ref[:, pl.ds(at, 16), :].astype(F32)
        for s in range(2):
            block = both[:, s * 8 : (s + 1) * 8, :].reshape(128, 128)
            block = jnp.where(line < size_ref[first + s], block, 0.0)
            own_ref[s, :, n * 128 : (n + 1) * 128] = block.astype(BF16)


def combine(r_ref, op_ref, h, sector):
    base = (1 - sector) * (r_ref.shape[1] // 2)
    both = r_ref[:, pl.ds(pl.multiple_of(base + h * 16, 16), 16), :].astype(F32)
    pair = []
    for e in range(2):
        summed = both[:, e * 8 : (e + 1) * 8, :].reshape(128, 128)
        pair.append((op_ref[2 * h + e].astype(F32) + summed).astype(BF16))
    return pair


def inner(block, right):
    return jnp.dot(block, right, preferred_element_type=F32).astype(BF16)


def joined(parts, first, last):
    return jnp.concatenate([v[:, first:last] for v in parts], axis=1)


def stacked(parts, first):
    tall = [jnp.concatenate([v[:, first : first + 128], v[:, first + 128 : first + 256]], axis=0) for v in parts]
    return jnp.concatenate(tall, axis=1)


def product(left, right):
    return jnp.dot(left, right, preferred_element_type=F32)


def turned(pool_ref, s, states):
    blocks = [pool_ref[s, :, n * 128 : (n + 1) * 128].astype(F32).T for n in states]
    return jnp.concatenate(blocks, axis=1).astype(BF16)


def pool_kernel(own_ref, up_ref, pool_ref, early_ref):
    for s in range(2):
        pool_ref[s] = own_ref[s]
        pool_ref[2 + s] = up_ref[s]
        early_ref[1 + s] = up_ref[s, :, 384:]
    early_ref[0] = own_ref[1, :, 384:]
    early_ref[3] = turned(own_ref, 1, (3,))


def front(charge_ref, r_ref, op_ref, early_ref, out_ref):
    def step(h, _):
        pair = combine(r_ref, op_ref, h, 1)
        parts = [inner(pair[e], early_ref[charge_ref[2 * h + e]]) for e in range(2)]
        two = product(early_ref[3], joined(parts, 0, 128))
        for e in range(2):
            out_ref[2 * h + e] = two[:, e * 128 : (e + 1) * 128].astype(BF16)
        return 0

    lax.fori_loop(0, op_ref.shape[0] // 2, step, 0, unroll=12)


def front_far(*refs):
    @pl.when(lax.axis_index("core") == 1)
    def _():
        front(*refs)


def front_near(charge_ref, r_ref, op_ref, early_ref, came_ref, out_ref):
    @pl.when(lax.axis_index("core") == 0)
    def _():
        front(charge_ref, r_ref, op_ref, early_ref, out_ref)

    @pl.when(lax.axis_index("core") == 1)
    def _():
        out_ref[...] = came_ref[...]


def last_kernel(charge_ref, r_ref, zero_ref, one_ref, pool_ref, out_ref, comb_ref, other_ref, left_ref):
    left_ref[...] = jnp.concatenate([turned(pool_ref, 1, (1, 2)), turned(pool_ref, 0, (3,))], axis=1)

    def step(h, _):
        pair = combine(r_ref, zero_ref, h, 0)
        high = combine(r_ref, one_ref, h, 1)
        tall = []
        for e in range(2):
            k = 2 * h + e
            q = charge_ref[k]
            comb_ref[k], other_ref[k] = pair[e], high[e]
            ones = inner(high[e], pool_ref[q + 1, :, 128:384])
            two = inner(pair[e], pool_ref[q, :, 384:])
            tall.append(jnp.concatenate([ones[:, :128], ones[:, 128:], two], axis=0))
        total = product(left_ref[...], jnp.concatenate(tall, axis=1))
        for e in range(2):
            out_ref[2 * h + e] = total[:, e * 128 : (e + 1) * 128].astype(BF16)
        return 0

    lax.fori_loop(0, one_ref.shape[0] // 2, step, 0, unroll=6)


def own_kernel(charge_ref, one_ref, zero_ref, pool_ref, first_ref, second_ref, left_ref):
    left_ref[...] = jnp.concatenate([turned(pool_ref, 0, (0, 1, 2)), turned(pool_ref, 1, (0,))], axis=1)

    def step(h, _):
        low, high = [], []
        for e in range(2):
            k = 2 * h + e
            q = charge_ref[k]
            low.append(inner(zero_ref[k], pool_ref[q, :, :384]))
            high.append(inner(one_ref[k], pool_ref[q + 1, :, :128]))
        first = product(left_ref[:, :128], joined(low, 0, 128))
        second = product(left_ref[:, 128:384], stacked(low, 128)) + product(left_ref[:, 384:], joined(high, 0, 128))
        for e in range(2):
            k, at = 2 * h + e, slice(e * 128, (e + 1) * 128)
            first_ref[k] = first[:, at]
            second_ref[k] = second[:, at]
        return 0

    lax.fori_loop(0, one_ref.shape[0] // 2, step, 0, unroll=6)


def close(sector, kept_ref, came_ref, out_hbm, done_ref, sems):
    size = kept_ref.shape[0] // 3
    moves = []
    for piece in range(3):
        at = slice(piece * size, (piece + 1) * size)
        done_ref[at] = (kept_ref[at] + came_ref[at].astype(F32)).astype(BF16)
        moves.append(pltpu.make_async_copy(done_ref.at[at], out_hbm.at[at, sector], sems.at[piece]))
        moves[-1].start()
    for move in moves:
        move.wait()


def close_one(kept_ref, came_ref, out_hbm, done_ref, sems):
    close(1, kept_ref, came_ref, out_hbm, done_ref, sems)


def close_zero(kept_ref, came_ref, _, out_hbm, done_ref, sems):
    close(0, kept_ref, came_ref, out_hbm, done_ref, sems)


def body(site_tensor, operators, one_index, weights, comp_charge, one_charge, sector_size, coupling):
    ops = operators.shape[0]
    sds = jax.ShapeDtypeStruct
    column = jnp.concatenate([one_index.reshape(512, 128), site_tensor.reshape(16, 128)], axis=0)
    far = lax.all_gather(column, "zh", axis=0)
    coef = jnp.where(comp_charge[:, None] == one_charge[None, :], weights, jnp.zeros((), BF16))
    message = call(
        spread_kernel, sds((16, COEF_AT + ops, 128), BF16), [VMEM, VMEM], VMEM, [pltpu.VMEM((64, 128), F32)]
    )(coef, far)
    near = lax.all_to_all(message, PLANE, 0, 0, tiled=True)
    rows = ops * 8
    scratch = [pltpu.VMEM((2, 1024, 128), F32), pltpu.VMEM((2, 16 * rows, 128), F32)]
    flops = 2 * ops * 2 * 128**3
    half, wide, site = sds((ops, 128, 128), BF16), sds((ops, 128, 128), F32), sds((2, 128, 512), BF16)
    mixed = call(
        mix_kernel,
        pltpu.HBM((16, 2 * rows, 128), BF16),
        [VMEM],
        HBM,
        scratch + [pltpu.VMEM((16, 2 * rows, 128), BF16), DMA((2,))],
    )(near)
    landed = lax.all_to_all(mixed, PLANE, 0, 0, tiled=True)
    own = call(site_kernel, site, [SMEM, SMEM, VMEM], VMEM)(coupling, sector_size, near)
    upper = shift(own, -1)
    pool, early = call(
        pool_kernel, [sds((4, 128, 512), BF16), sds((4, 128, 128), BF16)], [VMEM] * 2, [VMEM] * 2
    )(own, upper)
    zero, one = operators[:, 0], operators[:, 1]
    onward = [(1, 3), (3, 5), (5, 7)]
    swap = [(i, i ^ 1) for i in range(8)]
    ins = [SMEM] + [VMEM] * 3
    leave = call(front_far, half, ins, VMEM, flops=flops)(comp_charge, landed, one, early)
    came = lax.ppermute(leave, GROUP, onward)
    leave, comb_zero, comb_one = call(
        last_kernel, [half] * 3, [SMEM] + [VMEM] * 4, [VMEM] * 3, [pltpu.VMEM((128, 384), BF16)], flops=3 * flops
    )(comp_charge, landed, zero, one, pool)
    came_zero = shift(leave, 1)
    near_one = call(front_near, half, ins + [VMEM], VMEM, flops=flops)(comp_charge, landed, one, early, came)
    came_one = lax.ppermute(near_one, GROUP, swap)
    first, second = call(
        own_kernel, [wide, wide], ins, [VMEM] * 2, [pltpu.VMEM((128, 512), BF16)], flops=4 * flops
    )(comp_charge, comb_one, comb_zero, pool)
    whole = sds((ops, 2, 128, 128), BF16)
    scratch = [pltpu.VMEM((ops, 128, 128), BF16), DMA((3,))]
    out = call(close_one, whole, [VMEM] * 2, HBM, scratch)(second, came_one)
    return call(close_zero, whole, [VMEM, VMEM, HBM], HBM, scratch, input_output_aliases={2: 0})(first, came_zero, out)


def solution(mesh):
    fine = Mesh(mesh.devices.reshape(4, 4, 4, 4, 2), ("x", "y", "zh", "zl", "core"))
    pair, sector = ("x", "y", "zh"), ("zl", "core")
    return jax.shard_map(
        body,
        mesh=fine,
        in_specs=(
            P(None, sector, pair, None),
            P(pair, sector, None, None),
            P(pair, sector, None, None),
            P(pair, None),
            P(pair),
            P(),
            P(),
            P(),
        ),
        out_specs=P(pair, sector, None, None),
        check_vma=False,
    )
```
